32 devices in a mesh: sec: 8 (over y, x, core), tile: 4 (over z).
Axes of the slice: x: 2, y: 2, z: 4, core: 2. Of those that a mesh axis runs over, the one named last changes fastest.
Arguments:
- section_image: bfloat16 [8, 2048, 1024], P('sec', 'tile')
- offsets: int32 [8, 4, 2], P('sec', 'tile'), may hold values from -16 to 16, as said below
- peak_shift: int32 [8, 16, 8, 2], P('sec', 'tile'), may hold values from -8 to 8
- accepted: int32 [8, 16, 8], P('sec', 'tile'), may hold values 0 or 1
Outputs:
- coarse_map: float32 [8, 512, 256], P('sec', 'tile')
- flow_map: float32 [8, 2048, 1024], P('sec', 'tile')
The draws below stay inside these ranges and needn't reach their ends.
Inputs may be any that keep to these rules, and one draw needn't show every extreme that they name: `offsets`: in every section some strip has row offset 16 and another strip row offset -16.
All inputs are finite; a program needn't handle non-finite values. No bound on the sum of `accepted` on one device may be relied on, other than what follows from the above.
Results may differ from the reference program's by a relative error of at most 0.0065.
Values may be sent and summed in bfloat16 or wider, within the bound.
A program may use at most 192 MiB of HBM per device.

```python
import math
import jax
import jax.numpy as jnp
from jax import lax

P_SIZE = 128
DS = 4
COARSE = 16
PEAK = 8
TH = 512
W = 1024
SECTIONS = 8
TILES = 4
H4 = 128
W4 = 256
NPR = 4
NPC = 8
RIM = 72


def draw_section_image(key, part):
    key_one, key_two, key_three = jax.random.split(key, 3)
    shape_all = (SECTIONS, TILES * TH, W)
    noise = jax.random.normal(key_one, shape_all, jnp.float32)
    row_scale = jnp.exp(jax.random.uniform(key_two, (SECTIONS, TILES * TH, 1), jnp.float32, 0.0, math.log(10.0)))
    col_scale = jnp.exp(jax.random.uniform(key_three, (SECTIONS, 1, W), jnp.float32, 0.0, math.log(10.0)))
    return (noise * row_scale * col_scale * 0.1).astype(jnp.bfloat16)


def draw_offsets(key, part):
    key_one, key_two = jax.random.split(jax.random.fold_in(key, 7), 2)
    draws_int = jax.random.randint(key_one, (SECTIONS, TILES, 2), -COARSE, COARSE + 1, dtype=jnp.int32)
    chosen = jax.random.randint(key_two, (SECTIONS, 1), 0, TILES, dtype=jnp.int32)
    counter = jnp.arange(TILES, dtype=jnp.int32)[None, :]
    row_shift = jnp.where(counter == chosen, COARSE, draws_int[:, :, 0])
    row_shift = jnp.where(counter == (chosen + 1) % TILES, -COARSE, row_shift)
    return jnp.stack([row_shift, draws_int[:, :, 1]], axis=2).astype(jnp.int32)


def set_ends(array, own_key, smallest, high):
    longest = array.shape.index(max(array.shape))
    spots = []
    for shift in (0, 1):
        where = [jax.random.randint(jax.random.fold_in(own_key, axis), (), 0, length) for axis, length in enumerate(array.shape)]
        where[longest] = (where[longest] + shift) % array.shape[longest]
        spots.append(tuple(where))
    return array.at[spots[0]].set(smallest).at[spots[1]].set(high)


def setup_inputs(seed: int = 0) -> dict:
    key_of = jax.random.split(jax.random.key(seed), 5)
    section_image = draw_section_image(jax.random.fold_in(key_of[4], 71), 0)
    offsets = draw_offsets(jax.random.fold_in(key_of[4], 71), 0)
    peak_shift = set_ends(jax.random.randint(key_of[2], (SECTIONS, TILES * NPR, NPC, 2), -PEAK, PEAK + 1), jax.random.fold_in(key_of[2], 1), -PEAK, PEAK).astype(jnp.int32)
    accepted = set_ends((jax.random.randint(key_of[3], (SECTIONS, TILES * NPR, NPC), 0, 4) < 3).astype(jnp.int32), jax.random.fold_in(key_of[3], 1), 0, 1)
    return {"section_image": section_image, "offsets": offsets, "peak_shift": peak_shift, "accepted": accepted}


epsilon = 1e-05

def shrink(field):
    return field.astype(jnp.float32).reshape(field.shape[0] // DS, DS, field.shape[1] // DS, DS).mean(axis=(1, 3)).astype(jnp.bfloat16)

def standardize(field):
    centre = lax.optimization_barrier(jnp.mean(field, axis=(1, 2), keepdims=True))
    centred = field - centre
    spread = lax.optimization_barrier(jnp.mean(centred * centred, axis=(1, 2), keepdims=True))
    return centred / jnp.sqrt(spread + epsilon)

def spectral_corr(left_side, right_side):
    left_spec = jnp.fft.fft2(left_side, axes=(1, 2))
    right_spec = jnp.fft.fft2(right_side, axes=(1, 2))
    return jnp.real(jnp.fft.ifft2(jnp.conj(left_spec) * right_spec, axes=(1, 2))).astype(jnp.float32)

def reference(section_image, offsets, peak_shift, accepted):
    previous_all = jnp.concatenate([jnp.zeros_like(section_image[:1]), section_image[:-1]], axis=0)

    def one_section(items):
        current, previous, tile_offs, peaks_here, keep_here = items
        small_now = shrink(current)
        small_prev = shrink(previous)
        padded_small = jnp.pad(small_prev, COARSE)
        own_small = small_now.reshape(TILES, H4, W4)
        tile_ids = jnp.arange(TILES, dtype=jnp.int32)

        def grab_small(tile_id, offset_pair):
            row_at = (tile_id * H4 + offset_pair[0] + COARSE).astype(jnp.int32)
            col_at = (offset_pair[1] + COARSE).astype(jnp.int32)
            return lax.dynamic_slice(padded_small, (row_at, col_at), (H4, W4))
        windows = jax.vmap(grab_small)(tile_ids, tile_offs)
        coarse = spectral_corr(standardize(own_small.astype(jnp.float32)), standardize(windows.astype(jnp.float32)))
        coarse_part = (coarse / math.sqrt(H4 * W4)).reshape(TILES * H4, W4)
        padded_full = jnp.pad(previous, RIM)
        own_patches = current.reshape(TILES * NPR, P_SIZE, NPC, P_SIZE).transpose(0, 2, 1, 3)
        row_offs = jnp.repeat(tile_offs[:, 0], NPR).astype(jnp.int32)
        col_offs = jnp.repeat(tile_offs[:, 1], NPR).astype(jnp.int32)
        row_base = (RIM + jnp.arange(TILES * NPR, dtype=jnp.int32)[:, None] * P_SIZE + DS * row_offs[:, None] + peaks_here[:, :, 0]).astype(jnp.int32)
        col_base = (RIM + jnp.arange(NPC, dtype=jnp.int32)[None, :] * P_SIZE + DS * col_offs[:, None] + peaks_here[:, :, 1]).astype(jnp.int32)

        def one_row(row_items):
            own_row, row_starts, col_starts, keep = row_items

            def grab(row_at, col_at):
                return lax.dynamic_slice(padded_full, (row_at, col_at), (P_SIZE, P_SIZE))
            windows_row = jax.vmap(grab)(row_starts, col_starts)
            result = spectral_corr(standardize(own_row.astype(jnp.float32)), standardize(windows_row.astype(jnp.float32)))
            return result / float(P_SIZE) * keep.astype(jnp.float32)[:, None, None]
        flows = lax.map(one_row, (own_patches, row_base, col_base, keep_here))
        flow_part = flows.transpose(0, 2, 1, 3).reshape(TILES * TH, W)
        return (coarse_part, flow_part)
    coarse_map, flow_map = lax.map(one_section, (section_image, previous_all, offsets, peak_shift, accepted))
    return (coarse_map, flow_map)
```

```python
import functools
import math

import jax
import jax.numpy as jnp
import ml_dtypes
import numpy as np
from jax import lax
from jax.experimental import pallas as pl
from jax.experimental.pallas import tpu as pltpu
from jax.sharding import PartitionSpec as P

P_SIZE = 128
DS = 4
COARSE = 16
RIM = 72
HALO = 80
LANES = 128
PAIR = 2 * P_SIZE
EPSILON = 1e-05
MESH = pl.DeviceIdType.MESH


def basis(n):
    half = n // 2
    y = np.arange(n)[:, None]
    f = np.arange(half)[None, :]
    angles = (y * f % n) * (2.0 * np.pi / n)
    cosines = np.cos(angles)
    sines = np.sin(angles)
    sines[:, 0] = np.where(y[:, 0] % 2 == 0, 1.0, -1.0)
    return cosines, sines


def weights(half):
    return np.where(np.arange(half) == 0, 1.0, 2.0)


def hi_lo(table):
    hi = table.astype(np.float32).astype(ml_dtypes.bfloat16)
    lo = (table - hi.astype(np.float64)).astype(np.float32).astype(ml_dtypes.bfloat16)
    return hi, lo


def col_table(n):
    cosines, sines = basis(n)
    half = n // 2
    count = PAIR // n
    out = np.zeros((PAIR, PAIR))
    for p in range(count):
        rows = slice(p * n, (p + 1) * n)
        out[rows, p * half : (p + 1) * half] = cosines
        out[rows, LANES + p * half : LANES + (p + 1) * half] = sines
    return out


def make_tables():
    cosines, sines = basis(P_SIZE)
    row = np.concatenate([cosines, sines], axis=1)
    row_weights = np.tile(weights(P_SIZE // 2), 2)
    forward_row = np.concatenate(hi_lo(row.T), axis=1)
    inverse_row = np.concatenate(hi_lo(row * row_weights[None, :] / P_SIZE), axis=1)
    forward_col = []
    inverse_col = []
    for n in (P_SIZE, PAIR):
        table = col_table(n)
        col_weights = np.tile(weights(n // 2), 2 * PAIR // n)
        forward_col.append(np.concatenate(hi_lo(table), axis=0))
        inverse_col.append(np.concatenate(hi_lo(table.T * col_weights[:, None] / n), axis=0))
    pool = (np.arange(512)[:, None] // DS == np.arange(128)[None, :]).astype(ml_dtypes.bfloat16)
    return forward_row, inverse_row, np.stack(forward_col), np.stack(inverse_col), pool


def mm(a, b):
    return jnp.dot(a, b, preferred_element_type=jnp.float32)


def normalized(block, scale=None):
    count = block.shape[0] * block.shape[1]
    centre = jnp.sum(block, axis=(0, 1), keepdims=True) * (1.0 / count)
    centred = block - centre
    spread = jnp.sum(centred * centred, axis=(0, 1), keepdims=True) * (1.0 / count)
    factor = 1.0 / jnp.sqrt(spread + EPSILON)
    if scale is not None:
        factor = factor * scale
    return (centred * factor).astype(jnp.bfloat16)


def forward(pair, row_table, col_tables):
    cols = mm(pair, col_tables[:PAIR]) + mm(pair, col_tables[PAIR:])
    cols = cols.astype(jnp.bfloat16)
    return mm(row_table, jnp.concatenate([cols, cols], axis=0))


def inverse_rows(product, row_table):
    product = product.astype(jnp.bfloat16)
    return mm(row_table, jnp.concatenate([product, product], axis=0)).astype(jnp.bfloat16)


def inverse_cols(rows, col_tables):
    return mm(rows, col_tables[:PAIR]) + mm(rows, col_tables[PAIR:])


def multiply(a, b, half):
    k = P_SIZE // 2
    row0 = lax.broadcasted_iota(jnp.int32, (k, LANES), 0) == 0
    lane0 = lax.broadcasted_iota(jnp.int32, (k, LANES), 1) % half == 0

    def quarters(z):
        return z[:k, :LANES], z[:k, LANES:], z[k:, :LANES], z[k:, LANES:]

    acc, acs, asc, ass = quarters(a)
    bcc, bcs, bsc, bss = quarters(b)

    def lanes(c, s):
        return c, jnp.where(lane0, 0.0, s), jnp.where(lane0, s, c)

    c_c, c_s, c_d = lanes(acc, acs)
    t_c, t_s, t_d = lanes(asc, ass)
    s_c, s_s, s_d = (jnp.where(row0, 0.0, t) for t in (t_c, t_s, t_d))
    d_c, d_s, d_d = (jnp.where(row0, t, c) for t, c in ((t_c, c_c), (t_s, c_s), (t_d, c_d)))
    out_cc = c_c * bcc + c_s * bcs + s_c * bsc + s_s * bss
    out_cs = c_d * bcs - c_s * bcc + s_d * bss - s_s * bsc
    out_sc = d_c * bsc + d_s * bss - s_c * bcc - s_s * bcs
    out_ss = d_d * bss - d_s * bsc - s_d * bcs + s_s * bcc
    top = jnp.concatenate([out_cc, out_cs], axis=1)
    bottom = jnp.concatenate([out_sc, out_ss], axis=1)
    return jnp.concatenate([top, bottom], axis=0)


def pooled(block, pool):
    count = block.shape[0] // DS
    target = lax.broadcasted_iota(jnp.int32, (count, DS * count), 0) * DS
    source = lax.broadcasted_iota(jnp.int32, (count, DS * count), 1)
    near = (source >= target) & (source < target + DS)
    rows = mm(jnp.where(near, 1.0 / (DS * DS), 0.0).astype(jnp.bfloat16), block)
    parts = []
    for at in range(0, block.shape[1], 512):
        part = rows[:, at : at + 512]
        hi = part.astype(jnp.bfloat16)
        lo = (part - hi.astype(jnp.float32)).astype(jnp.bfloat16)
        parts.append(mm(hi, pool) + mm(lo, pool))
    return jnp.concatenate(parts, axis=1).astype(jnp.bfloat16).astype(jnp.float32)


def chunk_list(rows):
    chunks = [(0, HALO), (rows - HALO, HALO)]
    at = HALO
    while at < rows - HALO:
        size = min(P_SIZE, rows - HALO - at)
        chunks.append((at, size))
        at += size
    return chunks


def exchange_kernel(
    chunks,
    bands,
    pairs,
    img,
    row_hbm,
    col_hbm,
    pool_hbm,
    ext,
    spec_out,
    own,
    spec,
    row_tab,
    col_tab,
    pool,
    send_sems,
    recv_sems,
    local_sems,
):
    s = lax.axis_index("sec")
    t = lax.axis_index("tile")
    ns = lax.axis_size("sec")
    nt = lax.axis_size("tile")
    rows = own.shape[0]
    n_chunks = len(chunks)

    loads = [
        pltpu.make_async_copy(img, own, local_sems.at[0]),
        pltpu.make_async_copy(row_hbm, row_tab, local_sems.at[1]),
        pltpu.make_async_copy(col_hbm, col_tab, local_sems.at[2]),
        pltpu.make_async_copy(pool_hbm, pool, local_sems.at[3]),
    ]
    for load in loads:
        load.start()

    sends = s < ns - 1
    receives = s > 0
    has_up = t > 0
    has_down = t < nt - 1
    s_next = jnp.minimum(s + 1, ns - 1)
    s_prev = jnp.maximum(s - 1, 0)
    t_next = jnp.minimum(t + 1, nt - 1)
    t_prev = jnp.maximum(t - 1, 0)

    barrier = pltpu.get_barrier_semaphore()
    for cond, peer in (
        (sends, (s_next, t)),
        (receives, (s_prev, t)),
        (has_up, (s, t_prev)),
        (has_down, (s, t_next)),
    ):

        @pl.when(cond)
        def _(peer=peer):
            pl.semaphore_signal(barrier, inc=1, device_id=peer, device_id_type=MESH)

    peers = sum(jnp.where(cond, 1, 0) for cond in (sends, receives, has_up, has_down))
    pl.semaphore_wait(barrier, peers)

    def main_copy(n):
        start, size = chunks[n]
        return pltpu.make_async_remote_copy(
            src_ref=img.at[pl.ds(start, size)],
            dst_ref=ext.at[pl.ds(HALO + start, size)],
            send_sem=send_sems.at[n],
            recv_sem=recv_sems.at[n],
            device_id=(s_next, t),
            device_id_type=MESH,
        )

    def up_copy():
        return pltpu.make_async_remote_copy(
            src_ref=ext.at[pl.ds(HALO, HALO)],
            dst_ref=ext.at[pl.ds(HALO + rows, HALO)],
            send_sem=send_sems.at[n_chunks],
            recv_sem=recv_sems.at[n_chunks],
            device_id=(s, t_prev),
            device_id_type=MESH,
        )

    def down_copy():
        return pltpu.make_async_remote_copy(
            src_ref=ext.at[pl.ds(rows, HALO)],
            dst_ref=ext.at[pl.ds(0, HALO)],
            send_sem=send_sems.at[n_chunks + 1],
            recv_sem=recv_sems.at[n_chunks + 1],
            device_id=(s, t_next),
            device_id_type=MESH,
        )

    @pl.when(sends)
    def _():
        for n in range(n_chunks):
            main_copy(n).start()

    for load in loads:
        load.wait()

    def band(i, carry):
        base = pl.multiple_of(i * P_SIZE, P_SIZE)
        for j in range(pairs):
            wide = own[pl.ds(base, P_SIZE), j * PAIR : (j + 1) * PAIR].astype(jnp.float32)
            pair = jnp.concatenate(
                [normalized(wide[:, :P_SIZE]), normalized(wide[:, P_SIZE:])], axis=1
            )
            spec[i * pairs + j] = forward(pair, row_tab[...], col_tab[0])
        return carry

    lax.fori_loop(0, bands // 2, band, 0)

    @pl.when(receives)
    def _():
        main_copy(0).wait_recv()

        @pl.when(has_up)
        def _():
            up_copy().start()

        main_copy(1).wait_recv()

        @pl.when(has_down)
        def _():
            down_copy().start()

    lax.fori_loop(bands // 2, bands, band, 0)
    small = pooled(own[...], pool[...])
    spec[bands * pairs] = forward(normalized(small), row_tab[...], col_tab[1])
    store = pltpu.make_async_copy(spec, spec_out, local_sems.at[0])
    store.start()

    @pl.when(receives)
    def _():
        for n in range(2, n_chunks):
            main_copy(n).wait_recv()

        @pl.when(has_up)
        def _():
            up_copy().wait_send()
            down_copy().wait_recv()

        @pl.when(has_down)
        def _():
            down_copy().wait_send()
            up_copy().wait_recv()

    @pl.when(sends)
    def _():
        for n in range(n_chunks):
            main_copy(n).wait_send()

    store.wait()


SUB = 8


def window_at(ref, row_at, col_at, height, width):
    row_block = pl.multiple_of(row_at // SUB * SUB, SUB)
    col_block = pl.multiple_of(col_at // LANES * LANES, LANES)
    row_shift = lax.rem(row_at, SUB)
    col_shift = lax.rem(col_at, LANES)
    wide = ref[pl.ds(row_block, height + SUB), pl.ds(col_block, width + LANES)]
    lane = lax.broadcasted_iota(jnp.int32, (height + SUB, LANES), 1)
    sublane = lax.broadcasted_iota(jnp.int32, (height // SUB, SUB, LANES), 1)
    turn_lanes = lax.rem(LANES - col_shift, LANES)
    turn_rows = lax.rem(SUB - row_shift, SUB)
    parts = []
    for at in range(0, width, LANES):
        left = wide[:, at : at + LANES]
        right = wide[:, at + LANES : at + 2 * LANES]
        part = pltpu.roll(jnp.where(lane >= col_shift, left, right), turn_lanes, 1)
        part = pltpu.roll(part.reshape(height // SUB + 1, SUB, LANES), turn_rows, 1)
        part = jnp.where(sublane < SUB - row_shift, part[:-1], part[1:])
        parts.append(part.reshape(height, LANES))
    return parts[0] if len(parts) == 1 else jnp.concatenate(parts, axis=1)


def match_kernel(
    pairs,
    nt,
    offsets,
    peaks,
    keep,
    ext,
    spec,
    row_tab,
    col_tab,
    inv_row,
    inv_col,
    pool,
    coarse_out,
    flow_out,
    ext32,
    small32,
):
    band = pl.program_id(0)
    s = lax.axis_index("sec")
    t = lax.axis_index("tile")
    width = ext.shape[1]
    rows = ext.shape[0] - 2 * HALO
    off_row = offsets[0, 0, 0]
    off_col = offsets[0, 0, 1]

    @pl.when(band == 0)
    def _():
        zero_cols = jnp.zeros((rows + 2 * HALO + SUB, LANES), jnp.float32)
        ext32[rows + 2 * HALO :, :] = jnp.zeros((SUB, width + 2 * LANES), jnp.float32)
        ext32[:, :LANES] = zero_cols
        ext32[:, LANES + width :] = zero_cols

        def fill(valid, start, size):
            @pl.when(valid)
            def _():
                ext32[start : start + size, LANES : LANES + width] = ext[
                    start : start + size, :
                ].astype(jnp.float32)

            @pl.when(jnp.logical_not(valid))
            def _():
                ext32[start : start + size, LANES : LANES + width] = jnp.zeros(
                    (size, width), jnp.float32
                )

        fill((s > 0) & (t > 0), 0, HALO)
        fill(s > 0, HALO, rows)
        fill((s > 0) & (t < nt - 1), HALO + rows, HALO)

        small_rows = rows // DS
        small_cols = width // DS
        all_rows = small_rows + 2 * COARSE
        side = jnp.zeros((all_rows + SUB, LANES), jnp.float32)
        small32[all_rows:, :] = jnp.zeros((SUB, small_cols + 2 * LANES), jnp.float32)
        small32[:, :LANES] = side
        small32[:, LANES + small_cols :] = side
        first = HALO - DS * COARSE
        inner = ext32[first : first + DS * all_rows, LANES : LANES + width]
        small32[:all_rows, LANES : LANES + small_cols] = pooled(inner.astype(jnp.bfloat16), pool[...])
        window = window_at(
            small32, off_row + COARSE, off_col + LANES, small_rows, small_cols
        )
        other = forward(
            normalized(window, 1.0 / math.sqrt(small_rows * small_cols)), row_tab[...], col_tab[1]
        )
        product = multiply(spec[pl.num_programs(0) * pairs], other, LANES)
        coarse_out[0] = inverse_cols(inverse_rows(product, inv_row[...]), inv_col[1])

    for j in range(pairs):
        halves = []
        for n in range(2):
            column = 2 * j + n
            row_at = HALO + band * P_SIZE + DS * off_row + peaks[0, band, 0, column]
            col_at = LANES + column * P_SIZE + DS * off_col + peaks[0, band, 1, column]
            window = window_at(ext32, row_at, col_at, P_SIZE, P_SIZE)
            halves.append(
                normalized(window, keep[0, band, column].astype(jnp.float32) * (1.0 / P_SIZE))
            )
        other = forward(jnp.concatenate(halves, axis=1), row_tab[...], col_tab[0])
        product = multiply(spec[band * pairs + j], other, P_SIZE // 2)
        flow_out[0, :, j * PAIR : (j + 1) * PAIR] = inverse_cols(
            inverse_rows(product, inv_row[...]), inv_col[0]
        )


def shards(nt, section_image, offsets, peak_shift, accepted):
    own = section_image[0]
    rows, width = own.shape
    bands = rows // P_SIZE
    pairs = width // PAIR
    forward_row, inverse_row, forward_col, inverse_col, pool = (jnp.asarray(x) for x in make_tables())
    chunks = chunk_list(rows)
    hbm = pl.BlockSpec(memory_space=pl.ANY)
    vmem = pl.BlockSpec(memory_space=pltpu.VMEM)
    smem = pl.BlockSpec(memory_space=pltpu.SMEM)
    units = bands * pairs + 1
    ext, spec = pl.pallas_call(
        functools.partial(exchange_kernel, chunks, bands, pairs),
        name="exchange",
        out_shape=(
            jax.ShapeDtypeStruct((rows + 2 * HALO, width), jnp.bfloat16),
            jax.ShapeDtypeStruct((units, P_SIZE, PAIR), jnp.float32),
        ),
        in_specs=[hbm] * 4,
        out_specs=(hbm, hbm),
        scratch_shapes=[
            pltpu.VMEM((rows, width), jnp.bfloat16),
            pltpu.VMEM((units, P_SIZE, PAIR), jnp.float32),
            pltpu.VMEM(forward_row.shape, jnp.bfloat16),
            pltpu.VMEM(forward_col.shape, jnp.bfloat16),
            pltpu.VMEM(pool.shape, jnp.bfloat16),
            pltpu.SemaphoreType.DMA((len(chunks) + 2,)),
            pltpu.SemaphoreType.DMA((len(chunks) + 2,)),
            pltpu.SemaphoreType.DMA((4,)),
        ],
        compiler_params=pltpu.CompilerParams(collective_id=0, has_side_effects=True),
    )(own, forward_row, forward_col, pool)

    def whole(shape):
        return pl.BlockSpec(
            shape, lambda i: (0,) * len(shape), pipeline_mode=pl.Buffered(1)
        )

    coarse_map, flow_map = pl.pallas_call(
        functools.partial(match_kernel, pairs, nt),
        name="match",
        grid=(bands,),
        out_shape=(
            jax.ShapeDtypeStruct((1, rows // DS, width // DS), jnp.float32),
            jax.ShapeDtypeStruct((1, rows, width), jnp.float32),
        ),
        in_specs=[smem, smem, smem]
        + [
            whole(x.shape)
            for x in (ext, spec, forward_row, forward_col, inverse_row, inverse_col, pool)
        ],
        out_specs=(
            pl.BlockSpec((1, rows // DS, width // DS), lambda i: (0, 0, 0)),
            pl.BlockSpec((1, P_SIZE, width), lambda i: (0, i, 0)),
        ),
        scratch_shapes=[
            pltpu.VMEM((rows + 2 * HALO + SUB, width + 2 * LANES), jnp.float32),
            pltpu.VMEM((rows // DS + 2 * COARSE + SUB, width // DS + 2 * LANES), jnp.float32),
        ],
        compiler_params=pltpu.CompilerParams(dimension_semantics=("arbitrary",)),
    )(offsets, jnp.swapaxes(peak_shift, 2, 3), accepted, ext, spec, forward_row, forward_col, inverse_row, inverse_col, pool)
    return coarse_map, flow_map


def solution(mesh):
    return jax.shard_map(
        functools.partial(shards, mesh.shape["tile"]),
        mesh=mesh,
        in_specs=(
            P("sec", "tile", None),
            P("sec", "tile", None),
            P("sec", "tile", None, None),
            P("sec", "tile", None),
        ),
        out_specs=(P("sec", "tile", None), P("sec", "tile", None)),
        check_vma=False,
    )
```

```python
import functools
import math

import jax
import jax.numpy as jnp
import ml_dtypes
import numpy as np
from jax import lax
from jax.experimental import pallas as pl
from jax.experimental.pallas import tpu as pltpu
from jax.sharding import PartitionSpec as P

P_SIZE = 128
DS = 4
COARSE = 16
RIM = 72
HALO = 80
LANES = 128
PAIR = 2 * P_SIZE
EPSILON = 1e-05
MESH = pl.DeviceIdType.MESH


def basis(n):
    half = n // 2
    y = np.arange(n)[:, None]
    f = np.arange(half)[None, :]
    angles = (y * f % n) * (2.0 * np.pi / n)
    cosines = np.cos(angles)
    sines = np.sin(angles)
    sines[:, 0] = np.where(y[:, 0] % 2 == 0, 1.0, -1.0)
    return cosines, sines


def weights(half):
    return np.where(np.arange(half) == 0, 1.0, 2.0)


def hi_lo(table):
    hi = table.astype(np.float32).astype(ml_dtypes.bfloat16)
    lo = (table - hi.astype(np.float64)).astype(np.float32).astype(ml_dtypes.bfloat16)
    return hi, lo


def col_table(n):
    cosines, sines = basis(n)
    half = n // 2
    count = PAIR // n
    out = np.zeros((PAIR, PAIR))
    for p in range(count):
        rows = slice(p * n, (p + 1) * n)
        out[rows, p * half : (p + 1) * half] = cosines
        out[rows, LANES + p * half : LANES + (p + 1) * half] = sines
    return out


def make_tables():
    cosines, sines = basis(P_SIZE)
    row = np.concatenate([cosines, sines], axis=1)
    row_weights = np.tile(weights(P_SIZE // 2), 2)
    forward_row = np.concatenate(hi_lo(row.T), axis=1)
    inverse_row = np.concatenate(hi_lo(row * row_weights[None, :] / P_SIZE), axis=1)
    forward_col = []
    inverse_col = []
    for n in (P_SIZE, PAIR):
        table = col_table(n)
        col_weights = np.tile(weights(n // 2), 2 * PAIR // n)
        forward_col.append(np.concatenate(hi_lo(table), axis=0))
        inverse_col.append(np.concatenate(hi_lo(table.T * col_weights[:, None] / n), axis=0))
    pool = (np.arange(512)[:, None] // DS == np.arange(128)[None, :]).astype(ml_dtypes.bfloat16)
    return forward_row, inverse_row, np.stack(forward_col), np.stack(inverse_col), pool


def mm(a, b):
    return jnp.dot(a, b, preferred_element_type=jnp.float32)


def normalized(blocks, scales=None):
    count = blocks[0].shape[0] * blocks[0].shape[1]
    centres = [jnp.sum(x, axis=(0, 1), keepdims=True) * (1.0 / count) for x in blocks]
    centred = [x - c for x, c in zip(blocks, centres)]
    spreads = [jnp.sum(x * x, axis=(0, 1), keepdims=True) * (1.0 / count) for x in centred]
    factors = [1.0 / jnp.sqrt(v + EPSILON) for v in spreads]
    if scales is not None:
        factors = [f * k for f, k in zip(factors, scales)]
    return [(x * f).astype(jnp.bfloat16) for x, f in zip(centred, factors)]


def across(stack, count):
    return jnp.concatenate([stack[n * P_SIZE : (n + 1) * P_SIZE] for n in range(count)], axis=1)


def along(row, count):
    return jnp.concatenate([row[:, n * PAIR : (n + 1) * PAIR] for n in range(count)], axis=0)


def forward(stack, count, row_table, col_tables):
    cols = mm(stack, col_tables[:PAIR]) + mm(stack, col_tables[PAIR:])
    cols = across(cols.astype(jnp.bfloat16), count)
    return mm(row_table, jnp.concatenate([cols, cols], axis=0))


def inverse(products, count, row_table, col_tables):
    wide = jnp.concatenate([x.astype(jnp.bfloat16) for x in products], axis=1)
    rows = mm(row_table, jnp.concatenate([wide, wide], axis=0)).astype(jnp.bfloat16)
    rows = along(rows, count)
    return mm(rows, col_tables[:PAIR]) + mm(rows, col_tables[PAIR:])


def multiply(a, b, half):
    k = P_SIZE // 2
    row0 = lax.broadcasted_iota(jnp.int32, (k, LANES), 0) == 0
    lane0 = lax.broadcasted_iota(jnp.int32, (k, LANES), 1) % half == 0

    def quarters(z):
        return z[:k, :LANES], z[:k, LANES:], z[k:, :LANES], z[k:, LANES:]

    acc, acs, asc, ass = quarters(a)
    bcc, bcs, bsc, bss = quarters(b)

    def lanes(c, s):
        return c, jnp.where(lane0, 0.0, s), jnp.where(lane0, s, c)

    c_c, c_s, c_d = lanes(acc, acs)
    t_c, t_s, t_d = lanes(asc, ass)
    s_c, s_s, s_d = (jnp.where(row0, 0.0, t) for t in (t_c, t_s, t_d))
    d_c, d_s, d_d = (jnp.where(row0, t, c) for t, c in ((t_c, c_c), (t_s, c_s), (t_d, c_d)))
    out_cc = c_c * bcc + c_s * bcs + s_c * bsc + s_s * bss
    out_cs = c_d * bcs - c_s * bcc + s_d * bss - s_s * bsc
    out_sc = d_c * bsc + d_s * bss - s_c * bcc - s_s * bcs
    out_ss = d_d * bss - d_s * bsc - s_d * bcs + s_s * bcc
    top = jnp.concatenate([out_cc, out_cs], axis=1)
    bottom = jnp.concatenate([out_sc, out_ss], axis=1)
    return jnp.concatenate([top, bottom], axis=0)


def pooled(block, pool):
    count = block.shape[0] // DS
    target = lax.broadcasted_iota(jnp.int32, (count, DS * count), 0) * DS
    source = lax.broadcasted_iota(jnp.int32, (count, DS * count), 1)
    near = (source >= target) & (source < target + DS)
    rows = mm(jnp.where(near, 1.0 / (DS * DS), 0.0).astype(jnp.bfloat16), block)
    parts = []
    for at in range(0, block.shape[1], 512):
        part = rows[:, at : at + 512]
        hi = part.astype(jnp.bfloat16)
        lo = (part - hi.astype(jnp.float32)).astype(jnp.bfloat16)
        parts.append(mm(hi, pool) + mm(lo, pool))
    return jnp.concatenate(parts, axis=1).astype(jnp.bfloat16).astype(jnp.float32)


def chunk_list(rows):
    chunks = [(0, HALO), (rows - HALO, HALO)]
    at = HALO
    while at < rows - HALO:
        size = min(P_SIZE, rows - HALO - at)
        chunks.append((at, size))
        at += size
    return chunks


def exchange_kernel(
    chunks,
    bands,
    pairs,
    img,
    row_hbm,
    col_hbm,
    pool_hbm,
    ext,
    spec_out,
    own,
    spec,
    row_tab,
    col_tab,
    pool,
    send_sems,
    recv_sems,
    local_sems,
):
    s = lax.axis_index("sec")
    t = lax.axis_index("tile")
    ns = lax.axis_size("sec")
    nt = lax.axis_size("tile")
    rows = own.shape[0]
    n_chunks = len(chunks)

    loads = [
        pltpu.make_async_copy(img, own, local_sems.at[0]),
        pltpu.make_async_copy(row_hbm, row_tab, local_sems.at[1]),
        pltpu.make_async_copy(col_hbm, col_tab, local_sems.at[2]),
        pltpu.make_async_copy(pool_hbm, pool, local_sems.at[3]),
    ]
    for load in loads:
        load.start()

    sends = s < ns - 1
    receives = s > 0
    has_up = t > 0
    has_down = t < nt - 1
    s_next = jnp.minimum(s + 1, ns - 1)
    s_prev = jnp.maximum(s - 1, 0)
    t_next = jnp.minimum(t + 1, nt - 1)
    t_prev = jnp.maximum(t - 1, 0)

    barrier = pltpu.get_barrier_semaphore()
    for cond, peer in (
        (sends, (s_next, t)),
        (receives, (s_prev, t)),
        (has_up, (s, t_prev)),
        (has_down, (s, t_next)),
    ):

        @pl.when(cond)
        def _(peer=peer):
            pl.semaphore_signal(barrier, inc=1, device_id=peer, device_id_type=MESH)

    peers = sum(jnp.where(cond, 1, 0) for cond in (sends, receives, has_up, has_down))
    pl.semaphore_wait(barrier, peers)

    def main_copy(n):
        start, size = chunks[n]
        return pltpu.make_async_remote_copy(
            src_ref=img.at[pl.ds(start, size)],
            dst_ref=ext.at[pl.ds(HALO + start, size)],
            send_sem=send_sems.at[n],
            recv_sem=recv_sems.at[n],
            device_id=(s_next, t),
            device_id_type=MESH,
        )

    def up_copy():
        return pltpu.make_async_remote_copy(
            src_ref=ext.at[pl.ds(HALO, HALO)],
            dst_ref=ext.at[pl.ds(HALO + rows, HALO)],
            send_sem=send_sems.at[n_chunks],
            recv_sem=recv_sems.at[n_chunks],
            device_id=(s, t_prev),
            device_id_type=MESH,
        )

    def down_copy():
        return pltpu.make_async_remote_copy(
            src_ref=ext.at[pl.ds(rows, HALO)],
            dst_ref=ext.at[pl.ds(0, HALO)],
            send_sem=send_sems.at[n_chunks + 1],
            recv_sem=recv_sems.at[n_chunks + 1],
            device_id=(s, t_next),
            device_id_type=MESH,
        )

    @pl.when(sends)
    def _():
        for n in range(n_chunks):
            main_copy(n).start()

    for load in loads:
        load.wait()

    def band(i, carry):
        base = pl.multiple_of(i * P_SIZE, P_SIZE)
        wide = own[pl.ds(base, P_SIZE), :].astype(jnp.float32)
        flat = normalized([wide[:, n * P_SIZE : (n + 1) * P_SIZE] for n in range(2 * pairs)])
        stack = along(jnp.concatenate(flat, axis=1), pairs)
        spectra = forward(stack, pairs, row_tab[...], col_tab[0])
        for j in range(pairs):
            spec[i * pairs + j] = spectra[:, j * PAIR : (j + 1) * PAIR]
        return carry

    lax.fori_loop(0, bands // 2, band, 0)

    @pl.when(receives)
    def _():
        main_copy(0).wait_recv()

        @pl.when(has_up)
        def _():
            up_copy().start()

        main_copy(1).wait_recv()

        @pl.when(has_down)
        def _():
            down_copy().start()

    lax.fori_loop(bands // 2, bands, band, 0)
    small = pooled(own[...], pool[...])
    spec[bands * pairs] = forward(normalized([small])[0], 1, row_tab[...], col_tab[1])
    store = pltpu.make_async_copy(spec, spec_out, local_sems.at[0])
    store.start()

    @pl.when(receives)
    def _():
        for n in range(2, n_chunks):
            main_copy(n).wait_recv()

        @pl.when(has_up)
        def _():
            up_copy().wait_send()
            down_copy().wait_recv()

        @pl.when(has_down)
        def _():
            down_copy().wait_send()
            up_copy().wait_recv()

    @pl.when(sends)
    def _():
        for n in range(n_chunks):
            main_copy(n).wait_send()

    store.wait()


SUB = 8


def window_at(ref, row_at, col_at, height, width):
    row_block = pl.multiple_of(row_at // SUB * SUB, SUB)
    col_block = pl.multiple_of(col_at // LANES * LANES, LANES)
    row_shift = lax.rem(row_at, SUB)
    col_shift = lax.rem(col_at, LANES)
    wide = ref[pl.ds(row_block, height + SUB), pl.ds(col_block, width + LANES)]
    lane = lax.broadcasted_iota(jnp.int32, (height + SUB, LANES), 1)
    sublane = lax.broadcasted_iota(jnp.int32, (height // SUB, SUB, LANES), 1)
    turn_lanes = lax.rem(LANES - col_shift, LANES)
    turn_rows = lax.rem(SUB - row_shift, SUB)
    parts = []
    for at in range(0, width, LANES):
        left = wide[:, at : at + LANES]
        right = wide[:, at + LANES : at + 2 * LANES]
        part = pltpu.roll(jnp.where(lane >= col_shift, left, right), turn_lanes, 1)
        part = pltpu.roll(part.reshape(height // SUB + 1, SUB, LANES), turn_rows, 1)
        part = jnp.where(sublane < SUB - row_shift, part[:-1], part[1:])
        parts.append(part.reshape(height, LANES))
    return parts[0] if len(parts) == 1 else jnp.concatenate(parts, axis=1)


def match_kernel(
    pairs,
    nt,
    offsets,
    peaks,
    keep,
    ext,
    spec,
    row_tab,
    col_tab,
    inv_row,
    inv_col,
    pool,
    coarse_out,
    flow_out,
    ext32,
    small32,
):
    band = pl.program_id(0)
    s = lax.axis_index("sec")
    t = lax.axis_index("tile")
    width = ext.shape[1]
    rows = ext.shape[0] - 2 * HALO
    off_row = offsets[0, 0, 0]
    off_col = offsets[0, 0, 1]

    @pl.when(band == 0)
    def _():
        zero_cols = jnp.zeros((rows + 2 * HALO + SUB, LANES), jnp.float32)
        ext32[rows + 2 * HALO :, :] = jnp.zeros((SUB, width + 2 * LANES), jnp.float32)
        ext32[:, :LANES] = zero_cols
        ext32[:, LANES + width :] = zero_cols

        def fill(valid, start, size):
            @pl.when(valid)
            def _():
                ext32[start : start + size, LANES : LANES + width] = ext[
                    start : start + size, :
                ].astype(jnp.float32)

            @pl.when(jnp.logical_not(valid))
            def _():
                ext32[start : start + size, LANES : LANES + width] = jnp.zeros(
                    (size, width), jnp.float32
                )

        fill((s > 0) & (t > 0), 0, HALO)
        fill(s > 0, HALO, rows)
        fill((s > 0) & (t < nt - 1), HALO + rows, HALO)

        small_rows = rows // DS
        small_cols = width // DS
        all_rows = small_rows + 2 * COARSE
        side = jnp.zeros((all_rows + SUB, LANES), jnp.float32)
        small32[all_rows:, :] = jnp.zeros((SUB, small_cols + 2 * LANES), jnp.float32)
        small32[:, :LANES] = side
        small32[:, LANES + small_cols :] = side
        first = HALO - DS * COARSE
        inner = ext32[first : first + DS * all_rows, LANES : LANES + width]
        small32[:all_rows, LANES : LANES + small_cols] = pooled(inner.astype(jnp.bfloat16), pool[...])
        window = window_at(
            small32, off_row + COARSE, off_col + LANES, small_rows, small_cols
        )
        flat = normalized([window], [1.0 / math.sqrt(small_rows * small_cols)])[0]
        other = forward(flat, 1, row_tab[...], col_tab[1])
        product = multiply(spec[pl.num_programs(0) * pairs], other, LANES)
        coarse_out[0] = inverse([product], 1, inv_row[...], inv_col[1])

    windows = []
    scales = []
    for column in range(2 * pairs):
        row_at = HALO + band * P_SIZE + DS * off_row + peaks[0, band, 0, column]
        col_at = LANES + column * P_SIZE + DS * off_col + peaks[0, band, 1, column]
        windows.append(window_at(ext32, row_at, col_at, P_SIZE, P_SIZE))
        scales.append(keep[0, band, column].astype(jnp.float32) * (1.0 / P_SIZE))
    flat = normalized(windows, scales)
    stack = along(jnp.concatenate(flat, axis=1), pairs)
    spectra = forward(stack, pairs, row_tab[...], col_tab[0])
    products = [
        multiply(spec[band * pairs + j], spectra[:, j * PAIR : (j + 1) * PAIR], P_SIZE // 2)
        for j in range(pairs)
    ]
    maps = inverse(products, pairs, inv_row[...], inv_col[0])
    for j in range(pairs):
        flow_out[0, :, j * PAIR : (j + 1) * PAIR] = maps[j * P_SIZE : (j + 1) * P_SIZE]


def shards(nt, section_image, offsets, peak_shift, accepted):
    own = section_image[0]
    rows, width = own.shape
    bands = rows // P_SIZE
    pairs = width // PAIR
    forward_row, inverse_row, forward_col, inverse_col, pool = (jnp.asarray(x) for x in make_tables())
    chunks = chunk_list(rows)
    hbm = pl.BlockSpec(memory_space=pl.ANY)
    vmem = pl.BlockSpec(memory_space=pltpu.VMEM)
    smem = pl.BlockSpec(memory_space=pltpu.SMEM)
    units = bands * pairs + 1
    ext, spec = pl.pallas_call(
        functools.partial(exchange_kernel, chunks, bands, pairs),
        name="exchange",
        out_shape=(
            jax.ShapeDtypeStruct((rows + 2 * HALO, width), jnp.bfloat16),
            jax.ShapeDtypeStruct((units, P_SIZE, PAIR), jnp.float32),
        ),
        in_specs=[hbm] * 4,
        out_specs=(hbm, hbm),
        scratch_shapes=[
            pltpu.VMEM((rows, width), jnp.bfloat16),
            pltpu.VMEM((units, P_SIZE, PAIR), jnp.float32),
            pltpu.VMEM(forward_row.shape, jnp.bfloat16),
            pltpu.VMEM(forward_col.shape, jnp.bfloat16),
            pltpu.VMEM(pool.shape, jnp.bfloat16),
            pltpu.SemaphoreType.DMA((len(chunks) + 2,)),
            pltpu.SemaphoreType.DMA((len(chunks) + 2,)),
            pltpu.SemaphoreType.DMA((4,)),
        ],
        compiler_params=pltpu.CompilerParams(collective_id=0, has_side_effects=True),
    )(own, forward_row, forward_col, pool)

    def whole(shape):
        return pl.BlockSpec(
            shape, lambda i: (0,) * len(shape), pipeline_mode=pl.Buffered(1)
        )

    coarse_map, flow_map = pl.pallas_call(
        functools.partial(match_kernel, pairs, nt),
        name="match",
        grid=(bands,),
        out_shape=(
            jax.ShapeDtypeStruct((1, rows // DS, width // DS), jnp.float32),
            jax.ShapeDtypeStruct((1, rows, width), jnp.float32),
        ),
        in_specs=[smem, smem, smem]
        + [
            whole(x.shape)
            for x in (ext, spec, forward_row, forward_col, inverse_row, inverse_col, pool)
        ],
        out_specs=(
            pl.BlockSpec((1, rows // DS, width // DS), lambda i: (0, 0, 0)),
            pl.BlockSpec((1, P_SIZE, width), lambda i: (0, i, 0)),
        ),
        scratch_shapes=[
            pltpu.VMEM((rows + 2 * HALO + SUB, width + 2 * LANES), jnp.float32),
            pltpu.VMEM((rows // DS + 2 * COARSE + SUB, width // DS + 2 * LANES), jnp.float32),
        ],
        compiler_params=pltpu.CompilerParams(dimension_semantics=("arbitrary",)),
    )(offsets, jnp.swapaxes(peak_shift, 2, 3), accepted, ext, spec, forward_row, forward_col, inverse_row, inverse_col, pool)
    return coarse_map, flow_map


def solution(mesh):
    return jax.shard_map(
        functools.partial(shards, mesh.shape["tile"]),
        mesh=mesh,
        in_specs=(
            P("sec", "tile", None),
            P("sec", "tile", None),
            P("sec", "tile", None, None),
            P("sec", "tile", None),
        ),
        out_specs=(P("sec", "tile", None), P("sec", "tile", None)),
        check_vma=False,
    )
```

```python
import functools
import math

import jax
import jax.numpy as jnp
import ml_dtypes
import numpy as np
from jax import lax
from jax.experimental import pallas as pl
from jax.experimental.pallas import tpu as pltpu
from jax.sharding import PartitionSpec as P

P_SIZE = 128
DS = 4
COARSE = 16
RIM = 72
HALO = 80
LANES = 128
PAIR = 2 * P_SIZE
EPSILON = 1e-05
MESH = pl.DeviceIdType.MESH


def basis(n):
    half = n // 2
    y = np.arange(n)[:, None]
    f = np.arange(half)[None, :]
    angles = (y * f % n) * (2.0 * np.pi / n)
    cosines = np.cos(angles)
    sines = np.sin(angles)
    sines[:, 0] = np.where(y[:, 0] % 2 == 0, 1.0, -1.0)
    return cosines, sines


def weights(half):
    return np.where(np.arange(half) == 0, 1.0, 2.0)


def hi_lo(table):
    hi = table.astype(np.float32).astype(ml_dtypes.bfloat16)
    lo = (table - hi.astype(np.float64)).astype(np.float32).astype(ml_dtypes.bfloat16)
    return hi, lo


def col_table(n):
    cosines, sines = basis(n)
    half = n // 2
    count = PAIR // n
    out = np.zeros((PAIR, PAIR))
    for p in range(count):
        rows = slice(p * n, (p + 1) * n)
        out[rows, p * half : (p + 1) * half] = cosines
        out[rows, LANES + p * half : LANES + (p + 1) * half] = sines
    return out


def make_tables():
    cosines, sines = basis(P_SIZE)
    row = np.concatenate([cosines, sines], axis=1)
    row_weights = np.tile(weights(P_SIZE // 2), 2)
    forward_row = np.concatenate(hi_lo(row.T), axis=1)
    inverse_row = np.concatenate(hi_lo(row * row_weights[None, :] / P_SIZE), axis=1)
    forward_col = []
    inverse_col = []
    for n in (P_SIZE, PAIR):
        table = col_table(n)
        col_weights = np.tile(weights(n // 2), 2 * PAIR // n)
        forward_col.append(np.concatenate(hi_lo(table), axis=0))
        inverse_col.append(np.concatenate(hi_lo(table.T * col_weights[:, None] / n), axis=0))
    pool = (np.arange(512)[:, None] // DS == np.arange(128)[None, :]).astype(ml_dtypes.bfloat16)
    return forward_row, inverse_row, np.stack(forward_col), np.stack(inverse_col), pool


def mm(a, b):
    return jnp.dot(a, b, preferred_element_type=jnp.float32)


def normalized(blocks, scales=None):
    count = blocks[0].shape[0] * blocks[0].shape[1]
    centres = [jnp.sum(x, axis=(0, 1), keepdims=True) * (1.0 / count) for x in blocks]
    centred = [x - c for x, c in zip(blocks, centres)]
    spreads = [jnp.sum(x * x, axis=(0, 1), keepdims=True) * (1.0 / count) for x in centred]
    factors = [1.0 / jnp.sqrt(v + EPSILON) for v in spreads]
    if scales is not None:
        factors = [f * k for f, k in zip(factors, scales)]
    return [(x * f).astype(jnp.bfloat16) for x, f in zip(centred, factors)]


def across(stack, count):
    return jnp.concatenate([stack[n * P_SIZE : (n + 1) * P_SIZE] for n in range(count)], axis=1)


def along(row, count):
    return jnp.concatenate([row[:, n * PAIR : (n + 1) * PAIR] for n in range(count)], axis=0)


def forward(stack, count, row_table, col_tables):
    cols = mm(stack, col_tables[:PAIR]) + mm(stack, col_tables[PAIR:])
    cols = across(cols.astype(jnp.bfloat16), count)
    return mm(row_table, jnp.concatenate([cols, cols], axis=0))


def inverse(products, count, row_table, col_tables):
    wide = jnp.concatenate([x.astype(jnp.bfloat16) for x in products], axis=1)
    rows = mm(row_table, jnp.concatenate([wide, wide], axis=0)).astype(jnp.bfloat16)
    rows = along(rows, count)
    return mm(rows, col_tables[:PAIR]) + mm(rows, col_tables[PAIR:])


def multiply(a, b, half):
    k = P_SIZE // 2
    row0 = lax.broadcasted_iota(jnp.int32, (k, LANES), 0) == 0
    lane0 = lax.broadcasted_iota(jnp.int32, (k, LANES), 1) % half == 0

    def quarters(z):
        return z[:k, :LANES], z[:k, LANES:], z[k:, :LANES], z[k:, LANES:]

    acc, acs, asc, ass = quarters(a)
    bcc, bcs, bsc, bss = quarters(b)

    def lanes(c, s):
        return c, jnp.where(lane0, 0.0, s), jnp.where(lane0, s, c)

    c_c, c_s, c_d = lanes(acc, acs)
    t_c, t_s, t_d = lanes(asc, ass)
    s_c, s_s, s_d = (jnp.where(row0, 0.0, t) for t in (t_c, t_s, t_d))
    d_c, d_s, d_d = (jnp.where(row0, t, c) for t, c in ((t_c, c_c), (t_s, c_s), (t_d, c_d)))
    out_cc = c_c * bcc + c_s * bcs + s_c * bsc + s_s * bss
    out_cs = c_d * bcs - c_s * bcc + s_d * bss - s_s * bsc
    out_sc = d_c * bsc + d_s * bss - s_c * bcc - s_s * bcs
    out_ss = d_d * bss - d_s * bsc - s_d * bcs + s_s * bcc
    top = jnp.concatenate([out_cc, out_cs], axis=1)
    bottom = jnp.concatenate([out_sc, out_ss], axis=1)
    return jnp.concatenate([top, bottom], axis=0)


def pooled(block, pool):
    count = block.shape[0] // DS
    target = lax.broadcasted_iota(jnp.int32, (count, DS * count), 0) * DS
    source = lax.broadcasted_iota(jnp.int32, (count, DS * count), 1)
    near = (source >= target) & (source < target + DS)
    rows = mm(jnp.where(near, 1.0 / (DS * DS), 0.0).astype(jnp.bfloat16), block)
    parts = []
    for at in range(0, block.shape[1], 512):
        part = rows[:, at : at + 512]
        hi = part.astype(jnp.bfloat16)
        lo = (part - hi.astype(jnp.float32)).astype(jnp.bfloat16)
        parts.append(mm(hi, pool) + mm(lo, pool))
    return jnp.concatenate(parts, axis=1).astype(jnp.bfloat16).astype(jnp.float32)


def chunk_list(rows):
    chunks = [(0, HALO), (rows - HALO, HALO)]
    at = HALO
    while at < rows - HALO:
        size = min(P_SIZE, rows - HALO - at)
        chunks.append((at, size))
        at += size
    return chunks


def exchange_kernel(
    chunks,
    bands,
    pairs,
    img,
    row_hbm,
    col_hbm,
    pool_hbm,
    ext,
    spec_out,
    own,
    spec,
    row_tab,
    col_tab,
    pool,
    send_sems,
    recv_sems,
    local_sems,
):
    s = lax.axis_index("sec")
    t = lax.axis_index("tile")
    ns = lax.axis_size("sec")
    nt = lax.axis_size("tile")
    rows = own.shape[0]
    n_chunks = len(chunks)

    loads = [
        pltpu.make_async_copy(img, own, local_sems.at[0]),
        pltpu.make_async_copy(row_hbm, row_tab, local_sems.at[1]),
        pltpu.make_async_copy(col_hbm, col_tab, local_sems.at[2]),
        pltpu.make_async_copy(pool_hbm, pool, local_sems.at[3]),
    ]
    for load in loads:
        load.start()

    sends = s < ns - 1
    receives = s > 0
    has_up = t > 0
    has_down = t < nt - 1
    s_next = jnp.minimum(s + 1, ns - 1)
    s_prev = jnp.maximum(s - 1, 0)
    t_next = jnp.minimum(t + 1, nt - 1)
    t_prev = jnp.maximum(t - 1, 0)

    barrier = pltpu.get_barrier_semaphore()
    for cond, peer in (
        (sends, (s_next, t)),
        (receives, (s_prev, t)),
        (has_up, (s, t_prev)),
        (has_down, (s, t_next)),
    ):

        @pl.when(cond)
        def _(peer=peer):
            pl.semaphore_signal(barrier, inc=1, device_id=peer, device_id_type=MESH)

    peers = sum(jnp.where(cond, 1, 0) for cond in (sends, receives, has_up, has_down))
    pl.semaphore_wait(barrier, peers)

    def main_copy(n):
        start, size = chunks[n]
        return pltpu.make_async_remote_copy(
            src_ref=img.at[pl.ds(start, size)],
            dst_ref=ext.at[pl.ds(HALO + start, size)],
            send_sem=send_sems.at[n],
            recv_sem=recv_sems.at[n],
            device_id=(s_next, t),
            device_id_type=MESH,
        )

    def up_copy():
        return pltpu.make_async_remote_copy(
            src_ref=ext.at[pl.ds(HALO, HALO)],
            dst_ref=ext.at[pl.ds(HALO + rows, HALO)],
            send_sem=send_sems.at[n_chunks],
            recv_sem=recv_sems.at[n_chunks],
            device_id=(s, t_prev),
            device_id_type=MESH,
        )

    def down_copy():
        return pltpu.make_async_remote_copy(
            src_ref=ext.at[pl.ds(rows, HALO)],
            dst_ref=ext.at[pl.ds(0, HALO)],
            send_sem=send_sems.at[n_chunks + 1],
            recv_sem=recv_sems.at[n_chunks + 1],
            device_id=(s, t_next),
            device_id_type=MESH,
        )

    @pl.when(sends)
    def _():
        for n in range(n_chunks):
            main_copy(n).start()

    for load in loads:
        load.wait()

    def band(i, carry):
        base = pl.multiple_of(i * P_SIZE, P_SIZE)
        wide = own[pl.ds(base, P_SIZE), :].astype(jnp.float32)
        flat = normalized([wide[:, n * P_SIZE : (n + 1) * P_SIZE] for n in range(2 * pairs)])
        stack = along(jnp.concatenate(flat, axis=1), pairs)
        spectra = forward(stack, pairs, row_tab[...], col_tab[0])
        for j in range(pairs):
            spec[i * pairs + j] = spectra[:, j * PAIR : (j + 1) * PAIR]
        return carry

    lax.fori_loop(0, bands // 2, band, 0)

    @pl.when(receives)
    def _():
        main_copy(0).wait_recv()

        @pl.when(has_up)
        def _():
            up_copy().start()

        main_copy(1).wait_recv()

        @pl.when(has_down)
        def _():
            down_copy().start()

    lax.fori_loop(bands // 2, bands, band, 0)
    small = pooled(own[...], pool[...])
    spec[bands * pairs] = forward(normalized([small])[0], 1, row_tab[...], col_tab[1])
    store = pltpu.make_async_copy(spec, spec_out, local_sems.at[0])
    store.start()

    @pl.when(receives)
    def _():
        for n in range(2, n_chunks):
            main_copy(n).wait_recv()

        @pl.when(has_up)
        def _():
            up_copy().wait_send()
            down_copy().wait_recv()

        @pl.when(has_down)
        def _():
            down_copy().wait_send()
            up_copy().wait_recv()

    @pl.when(sends)
    def _():
        for n in range(n_chunks):
            main_copy(n).wait_send()

    store.wait()


SUB = 8


def window_at(ref, row_at, col_at, height, width):
    row_block = pl.multiple_of(row_at // SUB * SUB, SUB)
    col_block = pl.multiple_of(col_at // LANES * LANES, LANES)
    row_shift = lax.rem(row_at, SUB)
    col_shift = lax.rem(col_at, LANES)
    wide = ref[pl.ds(row_block, height + SUB), pl.ds(col_block, width + LANES)]
    lane = lax.broadcasted_iota(jnp.int32, (height + SUB, LANES), 1)
    sublane = lax.broadcasted_iota(jnp.int32, (height // SUB, SUB, LANES), 1)
    turn_lanes = lax.rem(LANES - col_shift, LANES)
    turn_rows = lax.rem(SUB - row_shift, SUB)
    parts = []
    for at in range(0, width, LANES):
        left = wide[:, at : at + LANES]
        right = wide[:, at + LANES : at + 2 * LANES]
        part = pltpu.roll(jnp.where(lane >= col_shift, left, right), turn_lanes, 1)
        part = pltpu.roll(part.reshape(height // SUB + 1, SUB, LANES), turn_rows, 1)
        part = jnp.where(sublane < SUB - row_shift, part[:-1], part[1:])
        parts.append(part.reshape(height, LANES))
    return parts[0] if len(parts) == 1 else jnp.concatenate(parts, axis=1)


def match_kernel(
    pairs,
    nt,
    offsets,
    peaks,
    keep,
    ext,
    spec,
    coarse_spec,
    row_tab,
    col_tab,
    inv_row,
    inv_col,
    pool,
    coarse_out,
    flow_out,
    ext32,
    small32,
):
    band = pl.program_id(0)
    s = lax.axis_index("sec")
    t = lax.axis_index("tile")
    width = ext.shape[1]
    rows = ext.shape[0] - 2 * HALO
    off_row = offsets[0, 0, 0]
    off_col = offsets[0, 0, 1]

    @pl.when(band == 0)
    def _():
        zero_cols = jnp.zeros((rows + 2 * HALO + SUB, LANES), jnp.float32)
        ext32[rows + 2 * HALO :, :] = jnp.zeros((SUB, width + 2 * LANES), jnp.float32)
        ext32[:, :LANES] = zero_cols
        ext32[:, LANES + width :] = zero_cols

        def fill(valid, start, size):
            @pl.when(valid)
            def _():
                ext32[start : start + size, LANES : LANES + width] = ext[
                    start : start + size, :
                ].astype(jnp.float32)

            @pl.when(jnp.logical_not(valid))
            def _():
                ext32[start : start + size, LANES : LANES + width] = jnp.zeros(
                    (size, width), jnp.float32
                )

        fill((s > 0) & (t > 0), 0, HALO)
        fill(s > 0, HALO, rows)
        fill((s > 0) & (t < nt - 1), HALO + rows, HALO)

        small_rows = rows // DS
        small_cols = width // DS
        all_rows = small_rows + 2 * COARSE
        side = jnp.zeros((all_rows + SUB, LANES), jnp.float32)
        small32[all_rows:, :] = jnp.zeros((SUB, small_cols + 2 * LANES), jnp.float32)
        small32[:, :LANES] = side
        small32[:, LANES + small_cols :] = side
        first = HALO - DS * COARSE
        inner = ext32[first : first + DS * all_rows, LANES : LANES + width]
        small32[:all_rows, LANES : LANES + small_cols] = pooled(inner.astype(jnp.bfloat16), pool[...])
        window = window_at(
            small32, off_row + COARSE, off_col + LANES, small_rows, small_cols
        )
        flat = normalized([window], [1.0 / math.sqrt(small_rows * small_cols)])[0]
        other = forward(flat, 1, row_tab[...], col_tab[1])
        product = multiply(coarse_spec[0], other, LANES)
        coarse_out[0] = inverse([product], 1, inv_row[...], inv_col[1])

    windows = []
    scales = []
    for column in range(2 * pairs):
        row_at = HALO + band * P_SIZE + DS * off_row + peaks[0, band, 0, column]
        col_at = LANES + column * P_SIZE + DS * off_col + peaks[0, band, 1, column]
        windows.append(window_at(ext32, row_at, col_at, P_SIZE, P_SIZE))
        scales.append(keep[0, band, column].astype(jnp.float32) * (1.0 / P_SIZE))
    flat = normalized(windows, scales)
    stack = along(jnp.concatenate(flat, axis=1), pairs)
    spectra = forward(stack, pairs, row_tab[...], col_tab[0])
    products = [
        multiply(spec[j], spectra[:, j * PAIR : (j + 1) * PAIR], P_SIZE // 2)
        for j in range(pairs)
    ]
    maps = inverse(products, pairs, inv_row[...], inv_col[0])
    for j in range(pairs):
        flow_out[0, :, j * PAIR : (j + 1) * PAIR] = maps[j * P_SIZE : (j + 1) * P_SIZE]


def shards(nt, section_image, offsets, peak_shift, accepted):
    own = section_image[0]
    rows, width = own.shape
    bands = rows // P_SIZE
    pairs = width // PAIR
    forward_row, inverse_row, forward_col, inverse_col, pool = (jnp.asarray(x) for x in make_tables())
    chunks = chunk_list(rows)
    hbm = pl.BlockSpec(memory_space=pl.ANY)
    vmem = pl.BlockSpec(memory_space=pltpu.VMEM)
    smem = pl.BlockSpec(memory_space=pltpu.SMEM)
    units = bands * pairs + 1
    ext, spec = pl.pallas_call(
        functools.partial(exchange_kernel, chunks, bands, pairs),
        name="exchange",
        out_shape=(
            jax.ShapeDtypeStruct((rows + 2 * HALO, width), jnp.bfloat16),
            jax.ShapeDtypeStruct((units, P_SIZE, PAIR), jnp.float32),
        ),
        in_specs=[hbm] * 4,
        out_specs=(hbm, hbm),
        scratch_shapes=[
            pltpu.VMEM((rows, width), jnp.bfloat16),
            pltpu.VMEM((units, P_SIZE, PAIR), jnp.float32),
            pltpu.VMEM(forward_row.shape, jnp.bfloat16),
            pltpu.VMEM(forward_col.shape, jnp.bfloat16),
            pltpu.VMEM(pool.shape, jnp.bfloat16),
            pltpu.SemaphoreType.DMA((len(chunks) + 2,)),
            pltpu.SemaphoreType.DMA((len(chunks) + 2,)),
            pltpu.SemaphoreType.DMA((4,)),
        ],
        compiler_params=pltpu.CompilerParams(collective_id=0, has_side_effects=True),
    )(own, forward_row, forward_col, pool)

    def whole(shape):
        return pl.BlockSpec(
            shape, lambda i: (0,) * len(shape), pipeline_mode=pl.Buffered(1)
        )

    coarse_map, flow_map = pl.pallas_call(
        functools.partial(match_kernel, pairs, nt),
        name="match",
        grid=(bands,),
        out_shape=(
            jax.ShapeDtypeStruct((1, rows // DS, width // DS), jnp.float32),
            jax.ShapeDtypeStruct((1, rows, width), jnp.float32),
        ),
        in_specs=[
            smem,
            smem,
            smem,
            whole(ext.shape),
            pl.BlockSpec((pairs, P_SIZE, PAIR), lambda i: (i, 0, 0)),
            pl.BlockSpec(
                (1, P_SIZE, PAIR), lambda i: (units - 1, 0, 0), pipeline_mode=pl.Buffered(1)
            ),
        ]
        + [
            whole(x.shape)
            for x in (forward_row, forward_col, inverse_row, inverse_col, pool)
        ],
        out_specs=(
            pl.BlockSpec((1, rows // DS, width // DS), lambda i: (0, 0, 0)),
            pl.BlockSpec((1, P_SIZE, width), lambda i: (0, i, 0)),
        ),
        scratch_shapes=[
            pltpu.VMEM((rows + 2 * HALO + SUB, width + 2 * LANES), jnp.float32),
            pltpu.VMEM((rows // DS + 2 * COARSE + SUB, width // DS + 2 * LANES), jnp.float32),
        ],
        compiler_params=pltpu.CompilerParams(dimension_semantics=("arbitrary",)),
    )(offsets, jnp.swapaxes(peak_shift, 2, 3), accepted, ext, spec, spec, forward_row, forward_col, inverse_row, inverse_col, pool)
    return coarse_map, flow_map


def solution(mesh):
    return jax.shard_map(
        functools.partial(shards, mesh.shape["tile"]),
        mesh=mesh,
        in_specs=(
            P("sec", "tile", None),
            P("sec", "tile", None),
            P("sec", "tile", None, None),
            P("sec", "tile", None),
        ),
        out_specs=(P("sec", "tile", None), P("sec", "tile", None)),
        check_vma=False,
    )
```

```python
import functools
import math

import jax
import jax.numpy as jnp
import ml_dtypes
import numpy as np
from jax import lax
from jax.experimental import pallas as pl
from jax.experimental.pallas import tpu as pltpu
from jax.sharding import PartitionSpec as P

P_SIZE = 128
DS = 4
COARSE = 16
RIM = 72
HALO = 80
LANES = 128
PAIR = 2 * P_SIZE
EPSILON = 1e-05
MESH = pl.DeviceIdType.MESH


def basis(n):
    half = n // 2
    y = np.arange(n)[:, None]
    f = np.arange(half)[None, :]
    angles = (y * f % n) * (2.0 * np.pi / n)
    cosines = np.cos(angles)
    sines = np.sin(angles)
    sines[:, 0] = np.where(y[:, 0] % 2 == 0, 1.0, -1.0)
    return cosines, sines


def weights(half):
    return np.where(np.arange(half) == 0, 1.0, 2.0)


def hi_lo(table):
    hi = table.astype(np.float32).astype(ml_dtypes.bfloat16)
    lo = (table - hi.astype(np.float64)).astype(np.float32).astype(ml_dtypes.bfloat16)
    return hi, lo


def col_table(n):
    cosines, sines = basis(n)
    half = n // 2
    count = PAIR // n
    out = np.zeros((PAIR, PAIR))
    for p in range(count):
        rows = slice(p * n, (p + 1) * n)
        out[rows, p * half : (p + 1) * half] = cosines
        out[rows, LANES + p * half : LANES + (p + 1) * half] = sines
    return out


def make_tables():
    cosines, sines = basis(P_SIZE)
    row = np.concatenate([cosines, sines], axis=1)
    row_weights = np.tile(weights(P_SIZE // 2), 2)
    forward_row = np.concatenate(hi_lo(row.T), axis=1)
    inverse_row = np.concatenate(hi_lo(row * row_weights[None, :] / P_SIZE), axis=1)
    forward_col = []
    inverse_col = []
    for n in (P_SIZE, PAIR):
        table = col_table(n)
        col_weights = np.tile(weights(n // 2), 2 * PAIR // n)
        forward_col.append(np.concatenate(hi_lo(table), axis=0))
        inverse_col.append(np.concatenate(hi_lo(table.T * col_weights[:, None] / n), axis=0))
    pool = (np.arange(512)[:, None] // DS == np.arange(128)[None, :]).astype(ml_dtypes.bfloat16)
    return forward_row, inverse_row, np.stack(forward_col), np.stack(inverse_col), pool


def mm(a, b):
    return jnp.dot(a, b, preferred_element_type=jnp.float32)


def normalized(blocks, scales=None):
    count = blocks[0].shape[0] * blocks[0].shape[1]
    centres = [jnp.sum(x, axis=(0, 1), keepdims=True) * (1.0 / count) for x in blocks]
    centred = [x - c for x, c in zip(blocks, centres)]
    spreads = [jnp.sum(x * x, axis=(0, 1), keepdims=True) * (1.0 / count) for x in centred]
    factors = [1.0 / jnp.sqrt(v + EPSILON) for v in spreads]
    if scales is not None:
        factors = [f * k for f, k in zip(factors, scales)]
    return [(x * f).astype(jnp.bfloat16) for x, f in zip(centred, factors)]


def across(stack, count):
    return jnp.concatenate([stack[n * P_SIZE : (n + 1) * P_SIZE] for n in range(count)], axis=1)


def along(row, count):
    return jnp.concatenate([row[:, n * PAIR : (n + 1) * PAIR] for n in range(count)], axis=0)


def forward(stack, count, row_table, col_tables):
    cols = mm(stack, col_tables[:PAIR]) + mm(stack, col_tables[PAIR:])
    cols = across(cols.astype(jnp.bfloat16), count)
    return mm(row_table, jnp.concatenate([cols, cols], axis=0))


def inverse(products, count, row_table, col_tables):
    wide = jnp.concatenate([x.astype(jnp.bfloat16) for x in products], axis=1)
    rows = mm(row_table, jnp.concatenate([wide, wide], axis=0)).astype(jnp.bfloat16)
    rows = along(rows, count)
    return mm(rows, col_tables[:PAIR]) + mm(rows, col_tables[PAIR:])


def multiply(a, b, half):
    k = P_SIZE // 2
    row0 = lax.broadcasted_iota(jnp.int32, (k, LANES), 0) == 0
    lane0 = lax.broadcasted_iota(jnp.int32, (k, LANES), 1) % half == 0

    def quarters(z):
        return z[:k, :LANES], z[:k, LANES:], z[k:, :LANES], z[k:, LANES:]

    acc, acs, asc, ass = quarters(a)
    bcc, bcs, bsc, bss = quarters(b)

    def lanes(c, s):
        return c, jnp.where(lane0, 0.0, s), jnp.where(lane0, s, c)

    c_c, c_s, c_d = lanes(acc, acs)
    t_c, t_s, t_d = lanes(asc, ass)
    s_c, s_s, s_d = (jnp.where(row0, 0.0, t) for t in (t_c, t_s, t_d))
    d_c, d_s, d_d = (jnp.where(row0, t, c) for t, c in ((t_c, c_c), (t_s, c_s), (t_d, c_d)))
    out_cc = c_c * bcc + c_s * bcs + s_c * bsc + s_s * bss
    out_cs = c_d * bcs - c_s * bcc + s_d * bss - s_s * bsc
    out_sc = d_c * bsc + d_s * bss - s_c * bcc - s_s * bcs
    out_ss = d_d * bss - d_s * bsc - s_d * bcs + s_s * bcc
    top = jnp.concatenate([out_cc, out_cs], axis=1)
    bottom = jnp.concatenate([out_sc, out_ss], axis=1)
    return jnp.concatenate([top, bottom], axis=0)


def pooled(block, pool):
    count = block.shape[0] // DS
    target = lax.broadcasted_iota(jnp.int32, (count, DS * count), 0) * DS
    source = lax.broadcasted_iota(jnp.int32, (count, DS * count), 1)
    near = (source >= target) & (source < target + DS)
    rows = mm(jnp.where(near, 1.0 / (DS * DS), 0.0).astype(jnp.bfloat16), block)
    parts = []
    for at in range(0, block.shape[1], 512):
        part = rows[:, at : at + 512]
        hi = part.astype(jnp.bfloat16)
        lo = (part - hi.astype(jnp.float32)).astype(jnp.bfloat16)
        parts.append(mm(hi, pool) + mm(lo, pool))
    return jnp.concatenate(parts, axis=1).astype(jnp.bfloat16).astype(jnp.float32)


def chunk_list(rows):
    chunks = [(0, HALO), (rows - HALO, HALO)]
    at = HALO
    while at < rows - HALO:
        size = min(P_SIZE, rows - HALO - at)
        chunks.append((at, size))
        at += size
    return chunks


def exchange_kernel(
    chunks,
    bands,
    pairs,
    img,
    row_hbm,
    col_hbm,
    pool_hbm,
    ext,
    spec_out,
    own,
    spec,
    row_tab,
    col_tab,
    pool,
    send_sems,
    recv_sems,
    local_sems,
):
    s = lax.axis_index("sec")
    t = lax.axis_index("tile")
    ns = lax.axis_size("sec")
    nt = lax.axis_size("tile")
    rows = own.shape[0]
    n_chunks = len(chunks)

    loads = [
        pltpu.make_async_copy(img, own, local_sems.at[0]),
        pltpu.make_async_copy(row_hbm, row_tab, local_sems.at[1]),
        pltpu.make_async_copy(col_hbm, col_tab, local_sems.at[2]),
        pltpu.make_async_copy(pool_hbm, pool, local_sems.at[3]),
    ]
    for load in loads:
        load.start()

    sends = s < ns - 1
    receives = s > 0
    has_up = t > 0
    has_down = t < nt - 1
    s_next = jnp.minimum(s + 1, ns - 1)
    s_prev = jnp.maximum(s - 1, 0)
    t_next = jnp.minimum(t + 1, nt - 1)
    t_prev = jnp.maximum(t - 1, 0)

    barrier = pltpu.get_barrier_semaphore()
    for cond, peer in (
        (sends, (s_next, t)),
        (receives, (s_prev, t)),
        (has_up, (s, t_prev)),
        (has_down, (s, t_next)),
    ):

        @pl.when(cond)
        def _(peer=peer):
            pl.semaphore_signal(barrier, inc=1, device_id=peer, device_id_type=MESH)

    peers = sum(jnp.where(cond, 1, 0) for cond in (sends, receives, has_up, has_down))
    pl.semaphore_wait(barrier, peers)

    def main_copy(n):
        start, size = chunks[n]
        return pltpu.make_async_remote_copy(
            src_ref=img.at[pl.ds(start, size)],
            dst_ref=ext.at[pl.ds(HALO + start, size)],
            send_sem=send_sems.at[n],
            recv_sem=recv_sems.at[n],
            device_id=(s_next, t),
            device_id_type=MESH,
        )

    def up_copy():
        return pltpu.make_async_remote_copy(
            src_ref=ext.at[pl.ds(HALO, HALO)],
            dst_ref=ext.at[pl.ds(HALO + rows, HALO)],
            send_sem=send_sems.at[n_chunks],
            recv_sem=recv_sems.at[n_chunks],
            device_id=(s, t_prev),
            device_id_type=MESH,
        )

    def down_copy():
        return pltpu.make_async_remote_copy(
            src_ref=ext.at[pl.ds(rows, HALO)],
            dst_ref=ext.at[pl.ds(0, HALO)],
            send_sem=send_sems.at[n_chunks + 1],
            recv_sem=recv_sems.at[n_chunks + 1],
            device_id=(s, t_next),
            device_id_type=MESH,
        )

    @pl.when(sends)
    def _():
        for n in range(n_chunks):
            main_copy(n).start()

    for load in loads:
        load.wait()

    def band(i, carry):
        base = pl.multiple_of(i * P_SIZE, P_SIZE)
        wide = own[pl.ds(base, P_SIZE), :].astype(jnp.float32)
        flat = normalized([wide[:, n * P_SIZE : (n + 1) * P_SIZE] for n in range(2 * pairs)])
        stack = along(jnp.concatenate(flat, axis=1), pairs)
        spectra = forward(stack, pairs, row_tab[...], col_tab[0])
        for j in range(pairs):
            spec[i * pairs + j] = spectra[:, j * PAIR : (j + 1) * PAIR]
        return carry

    lax.fori_loop(0, bands // 2, band, 0)

    @pl.when(receives)
    def _():
        main_copy(0).wait_recv()

        @pl.when(has_up)
        def _():
            up_copy().start()

        main_copy(1).wait_recv()

        @pl.when(has_down)
        def _():
            down_copy().start()

    lax.fori_loop(bands // 2, bands, band, 0)
    small = pooled(own[...], pool[...])
    spec[bands * pairs] = forward(normalized([small])[0], 1, row_tab[...], col_tab[1])
    store = pltpu.make_async_copy(spec, spec_out, local_sems.at[0])
    store.start()

    @pl.when(receives)
    def _():
        for n in range(2, n_chunks):
            main_copy(n).wait_recv()

        @pl.when(has_up)
        def _():
            up_copy().wait_send()
            down_copy().wait_recv()

        @pl.when(has_down)
        def _():
            down_copy().wait_send()
            up_copy().wait_recv()

    @pl.when(sends)
    def _():
        for n in range(n_chunks):
            main_copy(n).wait_send()

    store.wait()


SUB = 8


def window_at(ref, row_at, col_at, height, width):
    row_block = pl.multiple_of(row_at // SUB * SUB, SUB)
    col_block = pl.multiple_of(col_at // LANES * LANES, LANES)
    row_shift = lax.rem(row_at, SUB)
    col_shift = lax.rem(col_at, LANES)
    wide = ref[pl.ds(row_block, height + SUB), pl.ds(col_block, width + LANES)]
    lane = lax.broadcasted_iota(jnp.int32, (height + SUB, LANES), 1)
    sublane = lax.broadcasted_iota(jnp.int32, (height // SUB, SUB, LANES), 1)
    turn_lanes = lax.rem(LANES - col_shift, LANES)
    turn_rows = lax.rem(SUB - row_shift, SUB)
    parts = []
    for at in range(0, width, LANES):
        left = wide[:, at : at + LANES]
        right = wide[:, at + LANES : at + 2 * LANES]
        part = pltpu.roll(jnp.where(lane >= col_shift, left, right), turn_lanes, 1)
        part = pltpu.roll(part.reshape(height // SUB + 1, SUB, LANES), turn_rows, 1)
        part = jnp.where(sublane < SUB - row_shift, part[:-1], part[1:])
        parts.append(part.reshape(height, LANES))
    return parts[0] if len(parts) == 1 else jnp.concatenate(parts, axis=1)


def match_kernel(
    pairs,
    nt,
    offsets,
    peaks,
    keep,
    ext,
    spec,
    coarse_spec,
    row_tab,
    col_tab,
    inv_row,
    inv_col,
    pool,
    coarse_out,
    flow_out,
    ext32,
    small32,
):
    band = pl.program_id(0)
    s = lax.axis_index("sec")
    t = lax.axis_index("tile")
    width = ext.shape[1]
    rows = ext.shape[0] - 2 * HALO
    off_row = offsets[0, 0, 0]
    off_col = offsets[0, 0, 1]

    @pl.when(band == 0)
    def _():
        zero_cols = jnp.zeros((rows + 2 * HALO + SUB, LANES), jnp.float32)
        ext32[rows + 2 * HALO :, :] = jnp.zeros((SUB, width + 2 * LANES), jnp.float32)
        ext32[:, :LANES] = zero_cols
        ext32[:, LANES + width :] = zero_cols

        def fill(valid, start, size):
            @pl.when(valid)
            def _():
                ext32[start : start + size, LANES : LANES + width] = ext[
                    start : start + size, :
                ].astype(jnp.float32)

            @pl.when(jnp.logical_not(valid))
            def _():
                ext32[start : start + size, LANES : LANES + width] = jnp.zeros(
                    (size, width), jnp.float32
                )

        fill((s > 0) & (t > 0), 0, HALO)
        fill(s > 0, HALO, rows)
        fill((s > 0) & (t < nt - 1), HALO + rows, HALO)

        small_rows = rows // DS
        small_cols = width // DS
        all_rows = small_rows + 2 * COARSE
        side = jnp.zeros((all_rows + SUB, LANES), jnp.float32)
        small32[all_rows:, :] = jnp.zeros((SUB, small_cols + 2 * LANES), jnp.float32)
        small32[:, :LANES] = side
        small32[:, LANES + small_cols :] = side
        first = HALO - DS * COARSE
        inner = ext32[first : first + DS * all_rows, LANES : LANES + width]
        small32[:all_rows, LANES : LANES + small_cols] = pooled(inner.astype(jnp.bfloat16), pool[...])
        window = window_at(
            small32, off_row + COARSE, off_col + LANES, small_rows, small_cols
        )
        flat = normalized([window], [1.0 / math.sqrt(small_rows * small_cols)])[0]
        other = forward(flat, 1, row_tab[...], col_tab[1])
        product = multiply(coarse_spec[0], other, LANES)
        coarse_out[0] = inverse([product], 1, inv_row[...], inv_col[1])

    windows = []
    scales = []
    for column in range(2 * pairs):
        row_at = HALO + band * P_SIZE + DS * off_row + peaks[0, band, 0, column]
        col_at = LANES + column * P_SIZE + DS * off_col + peaks[0, band, 1, column]
        windows.append(window_at(ext32, row_at, col_at, P_SIZE, P_SIZE))
        scales.append(keep[0, band, column].astype(jnp.float32) * (1.0 / P_SIZE))
    flat = normalized(windows, scales)
    stack = along(jnp.concatenate(flat, axis=1), pairs)
    spectra = forward(stack, pairs, row_tab[...], col_tab[0])
    products = [
        multiply(spec[j], spectra[:, j * PAIR : (j + 1) * PAIR], P_SIZE // 2)
        for j in range(pairs)
    ]
    maps = inverse(products, pairs, inv_row[...], inv_col[0])
    for j in range(pairs):
        flow_out[0, :, j * PAIR : (j + 1) * PAIR] = maps[j * P_SIZE : (j + 1) * P_SIZE]


def shards(nt, section_image, offsets, peak_shift, accepted):
    own = section_image[0]
    rows, width = own.shape
    bands = rows // P_SIZE
    pairs = width // PAIR
    forward_row, inverse_row, forward_col, inverse_col, pool = (jnp.asarray(x) for x in make_tables())
    chunks = chunk_list(rows)
    hbm = pl.BlockSpec(memory_space=pl.ANY)
    vmem = pl.BlockSpec(memory_space=pltpu.VMEM)
    smem = pl.BlockSpec(memory_space=pltpu.SMEM)
    units = bands * pairs + 1
    ext, spec = pl.pallas_call(
        functools.partial(exchange_kernel, chunks, bands, pairs),
        name="exchange",
        out_shape=(
            jax.ShapeDtypeStruct((rows + 2 * HALO, width), jnp.bfloat16),
            jax.ShapeDtypeStruct((units, P_SIZE, PAIR), jnp.float32),
        ),
        in_specs=[pl.BlockSpec(memory_space=pltpu.HBM)] * 4,
        out_specs=(hbm, hbm),
        scratch_shapes=[
            pltpu.VMEM((rows, width), jnp.bfloat16),
            pltpu.VMEM((units, P_SIZE, PAIR), jnp.float32),
            pltpu.VMEM(forward_row.shape, jnp.bfloat16),
            pltpu.VMEM(forward_col.shape, jnp.bfloat16),
            pltpu.VMEM(pool.shape, jnp.bfloat16),
            pltpu.SemaphoreType.DMA((len(chunks) + 2,)),
            pltpu.SemaphoreType.DMA((len(chunks) + 2,)),
            pltpu.SemaphoreType.DMA((4,)),
        ],
        compiler_params=pltpu.CompilerParams(
            collective_id=0, has_side_effects=True, vmem_limit_bytes=16 * 2**20
        ),
    )(own, forward_row, forward_col, pool)

    def whole(shape):
        return pl.BlockSpec(
            shape, lambda i: (0,) * len(shape), pipeline_mode=pl.Buffered(1)
        )

    coarse_map, flow_map = pl.pallas_call(
        functools.partial(match_kernel, pairs, nt),
        name="match",
        grid=(bands,),
        out_shape=(
            jax.ShapeDtypeStruct((1, rows // DS, width // DS), jnp.float32),
            jax.ShapeDtypeStruct((1, rows, width), jnp.float32),
        ),
        in_specs=[
            smem,
            smem,
            smem,
            whole(ext.shape),
            pl.BlockSpec((pairs, P_SIZE, PAIR), lambda i: (i, 0, 0)),
            pl.BlockSpec(
                (1, P_SIZE, PAIR), lambda i: (units - 1, 0, 0), pipeline_mode=pl.Buffered(1)
            ),
        ]
        + [
            whole(x.shape)
            for x in (forward_row, forward_col, inverse_row, inverse_col, pool)
        ],
        out_specs=(
            pl.BlockSpec((1, rows // DS, width // DS), lambda i: (0, 0, 0)),
            pl.BlockSpec((1, P_SIZE, width), lambda i: (0, i, 0)),
        ),
        scratch_shapes=[
            pltpu.VMEM((rows + 2 * HALO + SUB, width + 2 * LANES), jnp.float32),
            pltpu.VMEM((rows // DS + 2 * COARSE + SUB, width // DS + 2 * LANES), jnp.float32),
        ],
        compiler_params=pltpu.CompilerParams(
            dimension_semantics=("arbitrary",), vmem_limit_bytes=24 * 2**20
        ),
    )(offsets, jnp.swapaxes(peak_shift, 2, 3), accepted, ext, spec, spec, forward_row, forward_col, inverse_row, inverse_col, pool)
    return coarse_map, flow_map


def solution(mesh):
    return jax.shard_map(
        functools.partial(shards, mesh.shape["tile"]),
        mesh=mesh,
        in_specs=(
            P("sec", "tile", None),
            P("sec", "tile", None),
            P("sec", "tile", None, None),
            P("sec", "tile", None),
        ),
        out_specs=(P("sec", "tile", None), P("sec", "tile", None)),
        check_vma=False,
    )
```

```python
import functools
import math

import jax
import jax.numpy as jnp
import ml_dtypes
import numpy as np
from jax import lax
from jax.experimental import pallas as pl
from jax.experimental.pallas import tpu as pltpu
from jax.sharding import PartitionSpec as P

P_SIZE = 128
DS = 4
COARSE = 16
RIM = 72
HALO = 80
LANES = 128
PAIR = 2 * P_SIZE
EPSILON = 1e-05
MESH = pl.DeviceIdType.MESH


def basis(n):
    half = n // 2
    y = np.arange(n)[:, None]
    f = np.arange(half)[None, :]
    angles = (y * f % n) * (2.0 * np.pi / n)
    cosines = np.cos(angles)
    sines = np.sin(angles)
    sines[:, 0] = np.where(y[:, 0] % 2 == 0, 1.0, -1.0)
    return cosines, sines


def weights(half):
    return np.where(np.arange(half) == 0, 1.0, 2.0)


def hi_lo(table):
    hi = table.astype(np.float32).astype(ml_dtypes.bfloat16)
    lo = (table - hi.astype(np.float64)).astype(np.float32).astype(ml_dtypes.bfloat16)
    return hi, lo


def col_table(n):
    cosines, sines = basis(n)
    half = n // 2
    count = PAIR // n
    out = np.zeros((PAIR, PAIR))
    for p in range(count):
        rows = slice(p * n, (p + 1) * n)
        out[rows, p * half : (p + 1) * half] = cosines
        out[rows, LANES + p * half : LANES + (p + 1) * half] = sines
    return out


def make_tables():
    cosines, sines = basis(P_SIZE)
    row = np.concatenate([cosines, sines], axis=1)
    row_weights = np.tile(weights(P_SIZE // 2), 2)
    forward_row = np.concatenate(hi_lo(row.T), axis=1)
    inverse_row = np.concatenate(hi_lo(row * row_weights[None, :] / P_SIZE), axis=1)
    forward_col = []
    inverse_col = []
    for n in (P_SIZE, PAIR):
        table = col_table(n)
        col_weights = np.tile(weights(n // 2), 2 * PAIR // n)
        forward_col.append(np.concatenate(hi_lo(table), axis=0))
        inverse_col.append(np.concatenate(hi_lo(table.T * col_weights[:, None] / n), axis=0))
    pool = (np.arange(512)[:, None] // DS == np.arange(128)[None, :]).astype(ml_dtypes.bfloat16)
    return forward_row, inverse_row, np.stack(forward_col), np.stack(inverse_col), pool


def mm(a, b):
    return jnp.dot(a, b, preferred_element_type=jnp.float32)


def normalized(blocks, scales=None):
    count = blocks[0].shape[0] * blocks[0].shape[1]
    centres = [jnp.sum(x, axis=(0, 1), keepdims=True) * (1.0 / count) for x in blocks]
    centred = [x - c for x, c in zip(blocks, centres)]
    spreads = [jnp.sum(x * x, axis=(0, 1), keepdims=True) * (1.0 / count) for x in centred]
    factors = [1.0 / jnp.sqrt(v + EPSILON) for v in spreads]
    if scales is not None:
        factors = [f * k for f, k in zip(factors, scales)]
    return [(x * f).astype(jnp.bfloat16) for x, f in zip(centred, factors)]


def across(stack, count):
    return jnp.concatenate([stack[n * P_SIZE : (n + 1) * P_SIZE] for n in range(count)], axis=1)


def along(row, count):
    return jnp.concatenate([row[:, n * PAIR : (n + 1) * PAIR] for n in range(count)], axis=0)


def forward(stack, count, row_table, col_tables):
    cols = mm(stack, col_tables[:PAIR]) + mm(stack, col_tables[PAIR:])
    cols = across(cols.astype(jnp.bfloat16), count)
    return mm(row_table, jnp.concatenate([cols, cols], axis=0))


def inverse(products, count, row_table, col_tables):
    wide = jnp.concatenate([x.astype(jnp.bfloat16) for x in products], axis=1)
    rows = mm(row_table, jnp.concatenate([wide, wide], axis=0)).astype(jnp.bfloat16)
    rows = along(rows, count)
    return mm(rows, col_tables[:PAIR]) + mm(rows, col_tables[PAIR:])


def multiply(a, b, half):
    k = P_SIZE // 2
    row0 = lax.broadcasted_iota(jnp.int32, (k, LANES), 0) == 0
    lane0 = lax.broadcasted_iota(jnp.int32, (k, LANES), 1) % half == 0

    def quarters(z):
        return z[:k, :LANES], z[:k, LANES:], z[k:, :LANES], z[k:, LANES:]

    acc, acs, asc, ass = quarters(a)
    bcc, bcs, bsc, bss = quarters(b)

    def lanes(c, s):
        return c, jnp.where(lane0, 0.0, s), jnp.where(lane0, s, c)

    c_c, c_s, c_d = lanes(acc, acs)
    t_c, t_s, t_d = lanes(asc, ass)
    s_c, s_s, s_d = (jnp.where(row0, 0.0, t) for t in (t_c, t_s, t_d))
    d_c, d_s, d_d = (jnp.where(row0, t, c) for t, c in ((t_c, c_c), (t_s, c_s), (t_d, c_d)))
    out_cc = c_c * bcc + c_s * bcs + s_c * bsc + s_s * bss
    out_cs = c_d * bcs - c_s * bcc + s_d * bss - s_s * bsc
    out_sc = d_c * bsc + d_s * bss - s_c * bcc - s_s * bcs
    out_ss = d_d * bss - d_s * bsc - s_d * bcs + s_s * bcc
    top = jnp.concatenate([out_cc, out_cs], axis=1)
    bottom = jnp.concatenate([out_sc, out_ss], axis=1)
    return jnp.concatenate([top, bottom], axis=0)


def pooled(block, pool):
    count = block.shape[0] // DS
    target = lax.broadcasted_iota(jnp.int32, (count, DS * count), 0) * DS
    source = lax.broadcasted_iota(jnp.int32, (count, DS * count), 1)
    near = (source >= target) & (source < target + DS)
    rows = mm(jnp.where(near, 1.0 / (DS * DS), 0.0).astype(jnp.bfloat16), block)
    parts = []
    for at in range(0, block.shape[1], 512):
        part = rows[:, at : at + 512]
        hi = part.astype(jnp.bfloat16)
        lo = (part - hi.astype(jnp.float32)).astype(jnp.bfloat16)
        parts.append(mm(hi, pool) + mm(lo, pool))
    return jnp.concatenate(parts, axis=1).astype(jnp.bfloat16).astype(jnp.float32)


def chunk_list(rows):
    chunks = [(0, HALO), (rows - HALO, HALO)]
    at = HALO
    while at < rows - HALO:
        size = min(P_SIZE, rows - HALO - at)
        chunks.append((at, size))
        at += size
    return chunks


def exchange_kernel(
    chunks,
    bands,
    pairs,
    img,
    row_hbm,
    col_hbm,
    pool_hbm,
    ext,
    spec_out,
    own,
    spec,
    row_tab,
    col_tab,
    pool,
    send_sems,
    recv_sems,
    local_sems,
):
    s = lax.axis_index("sec")
    t = lax.axis_index("tile")
    ns = lax.axis_size("sec")
    nt = lax.axis_size("tile")
    rows = own.shape[0]
    n_chunks = len(chunks)

    loads = [
        pltpu.make_async_copy(img, own, local_sems.at[0]),
        pltpu.make_async_copy(row_hbm, row_tab, local_sems.at[1]),
        pltpu.make_async_copy(col_hbm, col_tab, local_sems.at[2]),
        pltpu.make_async_copy(pool_hbm, pool, local_sems.at[3]),
    ]
    for load in loads:
        load.start()

    sends = s < ns - 1
    receives = s > 0
    has_up = t > 0
    has_down = t < nt - 1
    s_next = jnp.minimum(s + 1, ns - 1)
    s_prev = jnp.maximum(s - 1, 0)
    t_next = jnp.minimum(t + 1, nt - 1)
    t_prev = jnp.maximum(t - 1, 0)

    barrier = pltpu.get_barrier_semaphore()
    for cond, peer in (
        (sends, (s_next, t)),
        (receives, (s_prev, t)),
        (has_up, (s, t_prev)),
        (has_down, (s, t_next)),
    ):

        @pl.when(cond)
        def _(peer=peer):
            pl.semaphore_signal(barrier, inc=1, device_id=peer, device_id_type=MESH)

    peers = sum(jnp.where(cond, 1, 0) for cond in (sends, receives, has_up, has_down))
    pl.semaphore_wait(barrier, peers)

    def main_copy(n):
        start, size = chunks[n]
        return pltpu.make_async_remote_copy(
            src_ref=img.at[pl.ds(start, size)],
            dst_ref=ext.at[pl.ds(HALO + start, size)],
            send_sem=send_sems.at[n],
            recv_sem=recv_sems.at[n],
            device_id=(s_next, t),
            device_id_type=MESH,
        )

    def up_copy():
        return pltpu.make_async_remote_copy(
            src_ref=ext.at[pl.ds(HALO, HALO)],
            dst_ref=ext.at[pl.ds(HALO + rows, HALO)],
            send_sem=send_sems.at[n_chunks],
            recv_sem=recv_sems.at[n_chunks],
            device_id=(s, t_prev),
            device_id_type=MESH,
        )

    def down_copy():
        return pltpu.make_async_remote_copy(
            src_ref=ext.at[pl.ds(rows, HALO)],
            dst_ref=ext.at[pl.ds(0, HALO)],
            send_sem=send_sems.at[n_chunks + 1],
            recv_sem=recv_sems.at[n_chunks + 1],
            device_id=(s, t_next),
            device_id_type=MESH,
        )

    @pl.when(sends)
    def _():
        for n in range(n_chunks):
            main_copy(n).start()

    for load in loads:
        load.wait()

    def band(i, carry):
        base = pl.multiple_of(i * P_SIZE, P_SIZE)
        wide = own[pl.ds(base, P_SIZE), :].astype(jnp.float32)
        flat = normalized([wide[:, n * P_SIZE : (n + 1) * P_SIZE] for n in range(2 * pairs)])
        stack = along(jnp.concatenate(flat, axis=1), pairs)
        spectra = forward(stack, pairs, row_tab[...], col_tab[0])
        for j in range(pairs):
            spec[i * pairs + j] = spectra[:, j * PAIR : (j + 1) * PAIR]
        return carry

    lax.fori_loop(0, bands // 2, band, 0)

    @pl.when(receives)
    def _():
        main_copy(0).wait_recv()

        @pl.when(has_up)
        def _():
            up_copy().start()

        main_copy(1).wait_recv()

        @pl.when(has_down)
        def _():
            down_copy().start()

    lax.fori_loop(bands // 2, bands, band, 0)
    small = pooled(own[...], pool[...])
    spec[bands * pairs] = forward(normalized([small])[0], 1, row_tab[...], col_tab[1])
    store = pltpu.make_async_copy(spec, spec_out, local_sems.at[0])
    store.start()

    @pl.when(receives)
    def _():
        for n in range(2, n_chunks):
            main_copy(n).wait_recv()

        @pl.when(has_up)
        def _():
            up_copy().wait_send()
            down_copy().wait_recv()

        @pl.when(has_down)
        def _():
            down_copy().wait_send()
            up_copy().wait_recv()

    @pl.when(sends)
    def _():
        for n in range(n_chunks):
            main_copy(n).wait_send()

    store.wait()


SUB = 8


def window_at(ref, row_at, col_at, height, width):
    row_block = pl.multiple_of(row_at // SUB * SUB, SUB)
    col_block = pl.multiple_of(col_at // LANES * LANES, LANES)
    row_shift = lax.rem(row_at, SUB)
    col_shift = lax.rem(col_at, LANES)
    wide = ref[pl.ds(row_block, height + SUB), pl.ds(col_block, width + LANES)]
    lane = lax.broadcasted_iota(jnp.int32, (height + SUB, LANES), 1)
    sublane = lax.broadcasted_iota(jnp.int32, (height // SUB, SUB, LANES), 1)
    turn_lanes = lax.rem(LANES - col_shift, LANES)
    turn_rows = lax.rem(SUB - row_shift, SUB)
    parts = []
    for at in range(0, width, LANES):
        left = wide[:, at : at + LANES]
        right = wide[:, at + LANES : at + 2 * LANES]
        part = pltpu.roll(jnp.where(lane >= col_shift, left, right), turn_lanes, 1)
        part = pltpu.roll(part.reshape(height // SUB + 1, SUB, LANES), turn_rows, 1)
        part = jnp.where(sublane < SUB - row_shift, part[:-1], part[1:])
        parts.append(part.reshape(height, LANES))
    return parts[0] if len(parts) == 1 else jnp.concatenate(parts, axis=1)


def match_kernel(
    pairs,
    nt,
    offsets,
    peaks,
    keep,
    ext,
    spec,
    coarse_spec,
    row_tab,
    col_tab,
    inv_row,
    inv_col,
    pool,
    coarse_out,
    flow_out,
    ext32,
    small32,
):
    band = pl.program_id(0)
    s = lax.axis_index("sec")
    t = lax.axis_index("tile")
    width = ext.shape[1]
    rows = ext.shape[0] - 2 * HALO
    off_row = offsets[0, 0, 0]
    off_col = offsets[0, 0, 1]

    @pl.when(band == 0)
    def _():
        zero_cols = jnp.zeros((rows + 2 * HALO + SUB, LANES), jnp.float32)
        ext32[rows + 2 * HALO :, :] = jnp.zeros((SUB, width + 2 * LANES), jnp.float32)
        ext32[:, :LANES] = zero_cols
        ext32[:, LANES + width :] = zero_cols

        def fill(valid, start, size):
            @pl.when(valid)
            def _():
                ext32[start : start + size, LANES : LANES + width] = ext[
                    start : start + size, :
                ].astype(jnp.float32)

            @pl.when(jnp.logical_not(valid))
            def _():
                ext32[start : start + size, LANES : LANES + width] = jnp.zeros(
                    (size, width), jnp.float32
                )

        fill((s > 0) & (t > 0), 0, HALO)
        fill(s > 0, HALO, rows)
        fill((s > 0) & (t < nt - 1), HALO + rows, HALO)

        small_rows = rows // DS
        small_cols = width // DS
        all_rows = small_rows + 2 * COARSE
        side = jnp.zeros((all_rows + SUB, LANES), jnp.float32)
        small32[all_rows:, :] = jnp.zeros((SUB, small_cols + 2 * LANES), jnp.float32)
        small32[:, :LANES] = side
        small32[:, LANES + small_cols :] = side
        first = HALO - DS * COARSE
        inner = ext32[first : first + DS * all_rows, LANES : LANES + width]
        small32[:all_rows, LANES : LANES + small_cols] = pooled(inner.astype(jnp.bfloat16), pool[...])
        window = window_at(
            small32, off_row + COARSE, off_col + LANES, small_rows, small_cols
        )
        flat = normalized([window], [1.0 / math.sqrt(small_rows * small_cols)])[0]
        other = forward(flat, 1, row_tab[...], col_tab[1])
        product = multiply(coarse_spec[0], other, LANES)
        coarse_out[0] = inverse([product], 1, inv_row[...], inv_col[1])

    per = flow_out.shape[1] // P_SIZE
    windows = []
    scales = []
    for r in range(per):
        for column in range(2 * pairs):
            row = band * per + r
            row_at = HALO + row * P_SIZE + DS * off_row + peaks[0, row, 0, column]
            col_at = LANES + column * P_SIZE + DS * off_col + peaks[0, row, 1, column]
            windows.append(window_at(ext32, row_at, col_at, P_SIZE, P_SIZE))
            scales.append(keep[0, row, column].astype(jnp.float32) * (1.0 / P_SIZE))
    flat = normalized(windows, scales)
    count = per * pairs
    stack = along(jnp.concatenate(flat, axis=1), count)
    spectra = forward(stack, count, row_tab[...], col_tab[0])
    products = [
        multiply(spec[j], spectra[:, j * PAIR : (j + 1) * PAIR], P_SIZE // 2) for j in range(count)
    ]
    maps = inverse(products, count, inv_row[...], inv_col[0])
    for n in range(count):
        r, j = divmod(n, pairs)
        flow_out[0, r * P_SIZE : (r + 1) * P_SIZE, j * PAIR : (j + 1) * PAIR] = maps[
            n * P_SIZE : (n + 1) * P_SIZE
        ]


def shards(nt, section_image, offsets, peak_shift, accepted):
    own = section_image[0]
    rows, width = own.shape
    bands = rows // P_SIZE
    pairs = width // PAIR
    forward_row, inverse_row, forward_col, inverse_col, pool = (jnp.asarray(x) for x in make_tables())
    chunks = chunk_list(rows)
    hbm = pl.BlockSpec(memory_space=pl.ANY)
    vmem = pl.BlockSpec(memory_space=pltpu.VMEM)
    smem = pl.BlockSpec(memory_space=pltpu.SMEM)
    units = bands * pairs + 1
    per = 2 if bands % 2 == 0 else 1
    ext, spec = pl.pallas_call(
        functools.partial(exchange_kernel, chunks, bands, pairs),
        name="exchange",
        out_shape=(
            jax.ShapeDtypeStruct((rows + 2 * HALO, width), jnp.bfloat16),
            jax.ShapeDtypeStruct((units, P_SIZE, PAIR), jnp.float32),
        ),
        in_specs=[hbm] * 4,
        out_specs=(hbm, hbm),
        scratch_shapes=[
            pltpu.VMEM((rows, width), jnp.bfloat16),
            pltpu.VMEM((units, P_SIZE, PAIR), jnp.float32),
            pltpu.VMEM(forward_row.shape, jnp.bfloat16),
            pltpu.VMEM(forward_col.shape, jnp.bfloat16),
            pltpu.VMEM(pool.shape, jnp.bfloat16),
            pltpu.SemaphoreType.DMA((len(chunks) + 2,)),
            pltpu.SemaphoreType.DMA((len(chunks) + 2,)),
            pltpu.SemaphoreType.DMA((4,)),
        ],
        compiler_params=pltpu.CompilerParams(collective_id=0, has_side_effects=True),
    )(own, forward_row, forward_col, pool)

    def whole(shape):
        return pl.BlockSpec(
            shape, lambda i: (0,) * len(shape), pipeline_mode=pl.Buffered(1)
        )

    coarse_map, flow_map = pl.pallas_call(
        functools.partial(match_kernel, pairs, nt),
        name="match",
        grid=(bands // per,),
        out_shape=(
            jax.ShapeDtypeStruct((1, rows // DS, width // DS), jnp.float32),
            jax.ShapeDtypeStruct((1, rows, width), jnp.float32),
        ),
        in_specs=[
            smem,
            smem,
            smem,
            whole(ext.shape),
            pl.BlockSpec((per * pairs, P_SIZE, PAIR), lambda i: (i, 0, 0)),
            pl.BlockSpec(
                (1, P_SIZE, PAIR), lambda i: (units - 1, 0, 0), pipeline_mode=pl.Buffered(1)
            ),
        ]
        + [
            whole(x.shape)
            for x in (forward_row, forward_col, inverse_row, inverse_col, pool)
        ],
        out_specs=(
            pl.BlockSpec((1, rows // DS, width // DS), lambda i: (0, 0, 0)),
            pl.BlockSpec((1, per * P_SIZE, width), lambda i: (0, i, 0)),
        ),
        scratch_shapes=[
            pltpu.VMEM((rows + 2 * HALO + SUB, width + 2 * LANES), jnp.float32),
            pltpu.VMEM((rows // DS + 2 * COARSE + SUB, width // DS + 2 * LANES), jnp.float32),
        ],
        compiler_params=pltpu.CompilerParams(dimension_semantics=("arbitrary",)),
    )(offsets, jnp.swapaxes(peak_shift, 2, 3), accepted, ext, spec, spec, forward_row, forward_col, inverse_row, inverse_col, pool)
    return coarse_map, flow_map


def solution(mesh):
    return jax.shard_map(
        functools.partial(shards, mesh.shape["tile"]),
        mesh=mesh,
        in_specs=(
            P("sec", "tile", None),
            P("sec", "tile", None),
            P("sec", "tile", None, None),
            P("sec", "tile", None),
        ),
        out_specs=(P("sec", "tile", None), P("sec", "tile", None)),
        check_vma=False,
    )
```
